128 devices in a mesh: sec: 4 (over x), row: 32 (over y, z, core).
Axes of the slice: x: 4, y: 4, z: 4, core: 2. Of those that a mesh axis runs over, the one named last changes fastest.
Arguments:
- index_slices: float32 [4, 1024, 1024], P('sec', 'row'), may hold values from -6 to 6
- core_mask: int32 [1024, 1024], P('row'), may hold values 0 or 1
- illum_amp: float32 [1024, 1024], P('row'), may hold values from 0.5 to 1.5
- measured: float32 [8, 1024, 2, 1024], P(None, 'row'), may hold values from -6 to 6
- wave_ids: int32 [8], replicated, may hold values from 0 to 63
- angle_ids: int32 [8], replicated, may hold values from 0 to 63
Outputs:
- index_grad: float32 [4, 1024, 1024], P('sec', 'row')
The draws below stay inside these ranges and needn't reach their ends.
All inputs are finite; a program needn't handle non-finite values. No bound on the sum of `core_mask` on one device may be relied on, other than what follows from the above.
Results may differ from the reference program's by a relative error of at most 0.0003.
Values sent between devices are 32-bit elements; how exact they have to be, the bound alone decides.
No kernel may reach another device: no remote copies, remote signals or barrier semaphores. Data moves between devices by JAX's collectives and lax.ppermute only.
A program may use at most 256 MiB of HBM per device.

```python
import math
import jax
import jax.numpy as jnp

GRID = 1024
WAVES = 8
SLICES = 4
ANGLES = 64


def plant(entries, key, smallest, top_value):
    dims = entries.shape
    place = [jax.random.randint(jax.random.fold_in(key, axis), (), 0, dims[axis]) for axis in range(len(dims))]
    entries = entries.at[tuple(place)].set(smallest)
    longest = dims.index(max(dims))
    place[longest] = (place[longest] + 1) % dims[longest]
    return entries.at[tuple(place)].set(top_value)


def levels(key, shape, split, smallest, high):
    loudness, own = 1.0, jax.random.fold_in(key, 6)
    for dim, parts in split:
        heights = jnp.exp(jax.random.uniform(jax.random.fold_in(own, dim), (parts,), jnp.float32, smallest / len(split), high / len(split)))
        loudness = loudness * jnp.repeat(heights, shape[dim] // parts).reshape([-1 if axis == dim else 1 for axis in range(len(shape))])
    return loudness


def bell_draw(rng, shape, deviation, reach, split=(), kind=jnp.bfloat16):
    values = deviation * jax.random.normal(rng, shape, jnp.float32)
    if split:
        values = values * levels(rng, shape, split, -0.22, 0.18)
    return jnp.clip(values, -reach, reach).astype(kind)


def setup_inputs(seed: int = 0) -> dict:
    keys = jax.random.split(jax.random.key(seed), 7)
    return {
        "index_slices": bell_draw(keys[0], (SLICES, GRID, GRID), 1.0, 6.0, ((0, 4), (1, 32)), jnp.float32),
        "core_mask": plant((jax.random.randint(keys[1], (GRID, GRID), 0, 3) < 1).astype(jnp.int32), jax.random.fold_in(keys[1], 1), 0, 1),
        "illum_amp": jnp.clip(0.5 + 1.0 * jax.random.uniform(keys[2], (GRID, GRID), jnp.float32) ** levels(keys[2], (GRID, GRID), ((0, 32),), -0.2, 0.2), 0.5, 1.5),
        "measured": bell_draw(keys[3], (WAVES, GRID, 2, GRID), 1.0, 6.0, ((1, 32),), jnp.float32),
        "wave_ids": plant(jax.random.randint(keys[4], (WAVES,), 0, 64), jax.random.fold_in(keys[4], 1), 0, 63).astype(jnp.int32),
        "angle_ids": plant(jax.random.randint(keys[5], (WAVES,), 0, ANGLES), jax.random.fold_in(keys[5], 1), 0, ANGLES - 1).astype(jnp.int32),
    }


ratio_base = 0.75
ratio_step = 1.0 / 128.0
prop_scale = 150.0
core_step = 0.8
tilt_step = 8
angle_side = 8


def reference(index_slices, core_mask, illum_amp, measured, wave_ids, angle_ids):
    grid_size = core_mask.shape[0]
    positions = jnp.arange(grid_size, dtype=jnp.int32)
    signed = jnp.where(positions < grid_size // 2, positions, positions - grid_size)
    scaled = signed.astype(jnp.float32) / (grid_size // 2)
    squares = scaled * scaled
    freq_grid = squares[:, None] + squares[None, :]
    mask_float = core_mask.astype(jnp.float32)
    grad_list = [jnp.zeros((grid_size, grid_size), jnp.float32) for layer_index in range(SLICES)]
    for wave_index in range(WAVES):
        ratio_now = ratio_base + ratio_step * wave_ids[wave_index].astype(jnp.float32)
        propagator = jnp.exp(1j * ((-prop_scale * ratio_now) * freq_grid))
        angle_pick = angle_ids[wave_index]
        tilt_x = (angle_pick % angle_side - angle_side // 2) * tilt_step
        tilt_y = (angle_pick // angle_side - angle_side // 2) * tilt_step
        product = (tilt_x * positions[None, :] + tilt_y * positions[:, None]) % grid_size
        phase = (2.0 * math.pi / grid_size) * product.astype(jnp.float32)
        wave_field = illum_amp * jnp.exp(1j * phase)
        kept_fields = []
        for layer_index in range(SLICES):
            wave_field = jnp.fft.ifft2(propagator * jnp.fft.fft2(wave_field))
            phase_now = (core_step * mask_float + index_slices[layer_index]) / ratio_now
            wave_field = wave_field * jnp.exp(1j * phase_now)
            kept_fields.append(wave_field)
        adjoint = wave_field - (measured[wave_index, :, 0, :] + 1j * measured[wave_index, :, 1, :])
        for layer_index in reversed(range(SLICES)):
            forward_now = kept_fields[layer_index]
            term_now = (jnp.imag(adjoint) * jnp.real(forward_now) - jnp.real(adjoint) * jnp.imag(forward_now)) / ratio_now
            grad_list[layer_index] = grad_list[layer_index] + term_now
            phase_now = (core_step * mask_float + index_slices[layer_index]) / ratio_now
            adjoint = adjoint * jnp.exp(-1j * phase_now)
            adjoint = jnp.fft.ifft2(jnp.conj(propagator) * jnp.fft.fft2(adjoint))
    return jnp.stack(grad_list, axis=0).astype(jnp.float32)
```

```python
import functools
import math

import jax
import jax.numpy as jnp
import numpy as np
from jax import lax
from jax.experimental import pallas as pl
from jax.experimental.pallas import tpu as pltpu
from jax.sharding import PartitionSpec as P

ratio_base = 0.75
ratio_step = 1.0 / 128.0
prop_scale = 150.0
core_step = 0.8
tilt_step = 8
angle_side = 8

LANES = 128
GROUPS = 8
GRID = GROUPS * LANES
WIDE = 32
PEERS = GRID // WIDE
SHARE = 2
FOLD = LANES // WIDE
VMEM_LIMIT = 48 * 1024 * 1024


def dft_tables():
    counter = np.arange(LANES)
    angle = -2.0 * np.pi / LANES * (counter[:, None] * counter[None, :] % LANES)
    real, imag = np.cos(angle), np.sin(angle)
    full = np.block([[real, imag], [-imag, real]]).astype(np.float32)
    high = full.astype(jnp.bfloat16)
    low = (full - high.astype(np.float32)).astype(jnp.bfloat16)
    turn = -2.0 * np.pi / GRID * (np.arange(GROUPS)[:, None] * counter[None, :])
    twist = np.stack([np.cos(turn), np.sin(turn)]).astype(np.float32)
    return high, low, twist


def cos_sin(angle):
    turns = jnp.floor(angle * (2.0 / math.pi) + 0.5)
    rest = angle - turns * 1.5703125
    rest = rest - turns * 4.837512969970703e-4
    rest = rest - turns * 7.549789948768648e-8
    square = rest * rest
    sine = rest + rest * square * (
        -1.6666654611e-1 + square * (8.3321608736e-3 + square * -1.9515295891e-4)
    )
    cosine = (1.0 - 0.5 * square) + square * square * (
        4.166664568298827e-2 + square * (-1.388731625493765e-3 + square * 2.443315711809948e-5)
    )
    quarter = turns.astype(jnp.int32)
    swap = (quarter & 1) != 0
    cos_part = jnp.where(swap, sine, cosine)
    sin_part = jnp.where(swap, cosine, sine)
    cos_part = jnp.where(((quarter + 1) & 2) != 0, -cos_part, cos_part)
    sin_part = jnp.where((quarter & 2) != 0, -sin_part, sin_part)
    return cos_part, sin_part


def times(left, right):
    return (
        left[0] * right[0] - left[1] * right[1],
        left[0] * right[1] + left[1] * right[0],
    )


def times_conj(left, right):
    return (
        left[0] * right[0] + left[1] * right[1],
        left[1] * right[0] - left[0] * right[1],
    )


def plus(left, right):
    return (left[0] + right[0], left[1] + right[1])


def minus(left, right):
    return (left[0] - right[0], left[1] - right[1])


def quarter_turn(value, sign):
    if sign > 0:
        return (-value[1], value[0])
    return (value[1], -value[0])


def dft4(items, sign):
    even, odd = plus(items[0], items[2]), minus(items[0], items[2])
    other, rest = plus(items[1], items[3]), minus(items[1], items[3])
    rest = quarter_turn(rest, sign)
    return [plus(even, other), plus(odd, rest), minus(even, other), minus(odd, rest)]


def dft8(items, sign):
    even, odd = dft4(items[0::2], sign), dft4(items[1::2], sign)
    half = math.sqrt(0.5)
    first, third = odd[1], odd[3]
    if sign > 0:
        first = ((first[0] - first[1]) * half, (first[0] + first[1]) * half)
        third = ((-third[0] - third[1]) * half, (third[0] - third[1]) * half)
    else:
        first = ((first[0] + first[1]) * half, (first[1] - first[0]) * half)
        third = ((third[1] - third[0]) * half, (-third[0] - third[1]) * half)
    odd = [odd[0], first, quarter_turn(odd[2], sign), third]
    return [plus(e, o) for e, o in zip(even, odd)] + [minus(e, o) for e, o in zip(even, odd)]


def matmul_pair(left, right, high, low):
    both = jnp.concatenate([left, right], axis=1)
    upper = both.astype(jnp.bfloat16)
    lower = (both - upper.astype(jnp.float32)).astype(jnp.bfloat16)
    product = functools.partial(jnp.dot, preferred_element_type=jnp.float32)
    result = product(upper, high) + (product(lower, high) + product(upper, low))
    return result[:, :LANES], result[:, LANES:]


def line_filter(field, filters, twist, high, low, sign):
    stacked = []
    for wave in field:
        parts = dft8(wave, -1)
        stacked += [parts[0]] + [times(parts[k], twist[k]) for k in range(1, GROUPS)]
    real, imag = matmul_pair(
        jnp.concatenate([s[0] for s in stacked], axis=0),
        jnp.concatenate([s[1] for s in stacked], axis=0),
        high,
        low,
    )
    scaled = []
    for index in range(len(stacked)):
        rows = slice(index * WIDE, (index + 1) * WIDE)
        value, pick = (real[rows], imag[rows]), filters[index // GROUPS][index % GROUPS]
        scaled.append(times(value, pick) if sign > 0 else times_conj(value, pick))
    imag, real = matmul_pair(
        jnp.concatenate([s[1] for s in scaled], axis=0),
        jnp.concatenate([s[0] for s in scaled], axis=0),
        high,
        low,
    )
    result = []
    for wave in range(len(field)):
        parts = []
        for k in range(GROUPS):
            rows = slice((wave * GROUPS + k) * WIDE, (wave * GROUPS + k + 1) * WIDE)
            value = (real[rows], imag[rows])
            parts.append(value if k == 0 else times_conj(value, twist[k]))
        result.append(dft8(parts, 1))
    return result


def exchange_blocks(items):
    lane = lax.broadcasted_iota(jnp.int32, items[0].shape, items[0].ndim - 1)
    axis = items[0].ndim - 1
    low_half, even = (lane & 64) == 0, (lane & 32) == 0
    halves = [None] * 4
    for i in range(2):
        halves[i] = jnp.where(low_half, items[i], pltpu.roll(items[i + 2], 64, axis))
        halves[i + 2] = jnp.where(low_half, pltpu.roll(items[i], 64, axis), items[i + 2])
    result = [None] * 4
    for i in (0, 2):
        result[i] = jnp.where(even, halves[i], pltpu.roll(halves[i + 1], 32, axis))
        result[i + 1] = jnp.where(even, pltpu.roll(halves[i], LANES - 32, axis), halves[i + 1])
    return result


def load_field(blocks_ref):
    field = [[None] * GROUPS for _ in range(SHARE)]
    for group in range(GROUPS):
        items = exchange_blocks([blocks_ref[FOLD * group + i, :WIDE] for i in range(FOLD)])
        for wave in range(SHARE):
            field[wave][group] = (items[wave], items[SHARE + wave])
    return field


def store_field(blocks_ref, field):
    for group in range(GROUPS):
        rows = [field[w][group][part] for part in range(2) for w in range(SHARE)]
        turned = jnp.concatenate(rows, axis=0).T
        for i in range(FOLD):
            blocks_ref[FOLD * group + i, :WIDE] = turned[i * WIDE : (i + 1) * WIDE]


def pack_plane(plane):
    blocks = []
    for group in range(GROUPS):
        rows = [plane[group]] + [pltpu.roll(plane[group], LANES - 8 * q, 1) for q in range(1, FOLD)]
        turned = jnp.concatenate(rows, axis=0).T
        blocks += [turned[i * WIDE : i * WIDE + 8] for i in range(FOLD)]
    return blocks


def unpack_plane(blocks):
    plane = []
    for group in range(GROUPS):
        items = exchange_blocks(blocks[FOLD * group : FOLD * (group + 1)])
        plane.append(jnp.concatenate(items, axis=0))
    return plane


def ratio_of(place_ref, waves_ref, wave):
    number = waves_ref[place_ref[0] * SHARE + wave]
    return ratio_base + ratio_step * number.astype(jnp.float32)


def filters_of(place_ref, waves_ref):
    row = lax.broadcasted_iota(jnp.int32, (GROUPS, LANES), 0)
    lane = lax.broadcasted_iota(jnp.int32, (GROUPS, LANES), 1)
    natural = row + GROUPS * lane
    signed = jnp.where(natural < GRID // 2, natural, natural - GRID)
    scaled = signed.astype(jnp.float32) * (2.0 / GRID)
    squares = scaled * scaled
    filters = []
    for wave in range(SHARE):
        real, imag = cos_sin((-prop_scale * ratio_of(place_ref, waves_ref, wave)) * squares)
        real, imag = real * (1.0 / GRID), imag * (1.0 / GRID)
        filters.append([(real[k : k + 1], imag[k : k + 1]) for k in range(GROUPS)])
    return filters


def twist_of(twist_ref):
    return [(twist_ref[0, k : k + 1], twist_ref[1, k : k + 1]) for k in range(GROUPS)]


def inverse_ratio(place_ref, waves_ref, wave):
    ratio = ratio_of(place_ref, waves_ref, wave)
    return 1.0 / jnp.full((8, LANES), ratio, jnp.float32)[:1]


def launch_kernel(place_ref, waves_ref, angles_ref, illum_ref, high_ref, low_ref, twist_ref, out_ref):
    twist = twist_of(twist_ref)
    filters = filters_of(place_ref, waves_ref)
    field = []
    for wave in range(SHARE):
        pick = angles_ref[place_ref[0] * SHARE + wave]
        tilt_x = ((pick & (angle_side - 1)) - angle_side // 2) * tilt_step
        tilt_y = ((pick >> 3) - angle_side // 2) * tilt_step
        row = lax.broadcasted_iota(jnp.int32, (WIDE, LANES), 0) + place_ref[1] * WIDE

        def wheel(product):
            turned = ((product + GRID // 2) & (GRID - 1)) - GRID // 2
            return cos_sin((2.0 * math.pi / GRID) * turned.astype(jnp.float32))

        down = wheel(tilt_y * row)
        groups = []
        for group in range(GROUPS):
            column = lax.broadcasted_iota(jnp.int32, (8, LANES), 1) + group * LANES
            across = wheel(tilt_x * column)
            across = (across[0][:1], across[1][:1])
            wave_now = times(down, across)
            bright = illum_ref[:, group * LANES : (group + 1) * LANES]
            groups.append((bright * wave_now[0], bright * wave_now[1]))
        field.append(groups)
    field = line_filter(field, filters, twist, high_ref[...], low_ref[...], 1)
    store_field(out_ref, field)


def save(kept_ref, field):
    for wave in range(SHARE):
        for group in range(GROUPS):
            for part in range(2):
                kept_ref[wave, group, part] = field[wave][group][part]


def kept(kept_ref):
    return [
        [(kept_ref[wave, group, 0], kept_ref[wave, group, 1]) for group in range(GROUPS)]
        for wave in range(SHARE)
    ]


def read_base(base_ref, layer):
    if layer % 2:
        return [
            jnp.concatenate([base_ref[layer, tile * GROUPS + group] for tile in range(FOLD)], axis=0)
            for group in range(GROUPS)
        ]
    return unpack_plane([base_ref[layer, peer] for peer in range(PEERS)])


def screens(base_ref, layer, place_ref, waves_ref):
    base = read_base(base_ref, layer)
    result = []
    for wave in range(SHARE):
        scale = inverse_ratio(place_ref, waves_ref, wave)
        result.append([cos_sin(base[group] * scale) for group in range(GROUPS)])
    return result


def gradient(adjoint, field, place_ref, waves_ref):
    total = [None] * GROUPS
    for wave in range(SHARE):
        scale = inverse_ratio(place_ref, waves_ref, wave)
        for group in range(GROUPS):
            left, right = adjoint[wave][group], field[wave][group]
            term = (left[1] * right[0] - left[0] * right[1]) * scale
            total[group] = term if wave == 0 else total[group] + term
    return total


def each(function, left, right):
    return [[function(a, b) for a, b in zip(p, q)] for p, q in zip(left, right)]


def forward_kernel(
    layer, place_ref, waves_ref, in_ref, base_ref, high_ref, low_ref, twist_ref, out_ref, field_ref, screen_ref
):
    twist, high, low = twist_of(twist_ref), high_ref[...], low_ref[...]
    filters = filters_of(place_ref, waves_ref)
    field = line_filter(load_field(in_ref), filters, twist, high, low, 1)
    screen = screens(base_ref, layer, place_ref, waves_ref)
    save(screen_ref, screen)
    field = each(times, field, screen)
    save(field_ref, field)
    store_field(out_ref, line_filter(field, filters, twist, high, low, 1))


def turn_kernel(place_ref, waves_ref, in_ref, base_ref, target_ref, high_ref, low_ref, twist_ref, out_ref):
    twist, high, low = twist_of(twist_ref), high_ref[...], low_ref[...]
    filters = filters_of(place_ref, waves_ref)
    field = line_filter(load_field(in_ref), filters, twist, high, low, 1)
    screen = screens(base_ref, 3, place_ref, waves_ref)
    field = each(times, field, screen)
    adjoint = []
    for wave in range(SHARE):
        groups = []
        for group in range(GROUPS):
            lanes = slice(group * LANES, (group + 1) * LANES)
            goal = (target_ref[wave, :, 0, lanes], target_ref[wave, :, 1, lanes])
            groups.append(minus(field[wave][group], goal))
        adjoint.append(groups)
    blocks = pack_plane(gradient(adjoint, field, place_ref, waves_ref))
    for peer in range(PEERS):
        out_ref[peer, WIDE:] = blocks[peer]
    adjoint = each(times_conj, adjoint, screen)
    store_field(out_ref, line_filter(adjoint, filters, twist, high, low, -1))


def adjoint_kernel(
    with_plane, place_ref, waves_ref, in_ref, field_ref, screen_ref, high_ref, low_ref, twist_ref, out_ref, *grad_ref
):
    twist, high, low = twist_of(twist_ref), high_ref[...], low_ref[...]
    filters = filters_of(place_ref, waves_ref)
    adjoint = line_filter(load_field(in_ref), filters, twist, high, low, -1)
    grad = gradient(adjoint, kept(field_ref), place_ref, waves_ref)
    if with_plane:
        blocks = pack_plane(grad)
        for peer in range(PEERS):
            out_ref[peer, WIDE:] = blocks[peer]
    else:
        for group in range(GROUPS):
            grad_ref[0][group] = grad[group]
    adjoint = each(times_conj, adjoint, kept(screen_ref))
    store_field(out_ref, line_filter(adjoint, filters, twist, high, low, -1))


def last_kernel(
    place_ref, waves_ref, in_ref, field_ref, third_ref, second_ref, high_ref, low_ref, twist_ref, out_ref
):
    twist, high, low = twist_of(twist_ref), high_ref[...], low_ref[...]
    filters = filters_of(place_ref, waves_ref)
    adjoint = line_filter(load_field(in_ref), filters, twist, high, low, -1)
    planes = [
        gradient(adjoint, kept(field_ref), place_ref, waves_ref),
        unpack_plane([in_ref[peer, WIDE:] for peer in range(PEERS)]),
        [second_ref[group] for group in range(GROUPS)],
        unpack_plane([third_ref[peer, WIDE:] for peer in range(PEERS)]),
    ]
    for layer in range(4):
        blocks = pack_plane(planes[layer])
        for peer in range(PEERS):
            out_ref[layer * PEERS + peer] = blocks[peer]


def sum_kernel(in_ref, out_ref):
    total = [
        (in_ref[peer] + in_ref[PEERS + peer]) + (in_ref[2 * PEERS + peer] + in_ref[3 * PEERS + peer])
        for peer in range(PEERS)
    ]
    plane = unpack_plane(total)
    for group in range(GROUPS):
        out_ref[0, :, group * LANES : (group + 1) * LANES] = plane[group]


def base_kernel(slice_ref, mask_ref, rows_ref, out_ref):
    base = []
    for group in range(GROUPS):
        lanes = slice(group * LANES, (group + 1) * LANES)
        plane = core_step * mask_ref[:, lanes].astype(jnp.float32) + slice_ref[0, :, lanes]
        base.append(plane)
        for tile in range(FOLD):
            rows_ref[tile * GROUPS + group] = plane[tile * 8 : (tile + 1) * 8]
    blocks = pack_plane(base)
    for peer in range(PEERS):
        out_ref[peer] = blocks[peer]


def call(kernel, scalars, arrays, outs):
    specs = [pl.BlockSpec(memory_space=pltpu.SMEM)] * len(scalars)
    specs += [pl.BlockSpec(memory_space=pltpu.VMEM)] * len(arrays)
    return pl.pallas_call(
        kernel,
        out_shape=[jax.ShapeDtypeStruct(shape, jnp.float32) for shape in outs],
        in_specs=specs,
        out_specs=[pl.BlockSpec(memory_space=pltpu.VMEM)] * len(outs),
        compiler_params=pltpu.CompilerParams(vmem_limit_bytes=VMEM_LIMIT),
    )(*scalars, *arrays)


def body(index_slices, core_mask, illum_amp, measured, wave_ids, angle_ids):
    row_pos, sec_pos = lax.axis_index("row"), lax.axis_index("sec")
    high, low, twist = (jnp.asarray(table) for table in dft_tables())
    tables = (high, low, twist)
    place = jnp.stack([sec_pos, row_pos]).astype(jnp.int32)
    swap = functools.partial(lax.all_to_all, axis_name="row", split_axis=0, concat_axis=0, tiled=True)
    blocks, small = (PEERS, WIDE, LANES), (PEERS, 8, LANES)
    wide_blocks = (PEERS, WIDE + 8, LANES)
    saved = (SHARE, GROUPS, 2, WIDE, LANES)
    scalars = (place, wave_ids)

    base_rows, base_blocks = call(base_kernel, (), (index_slices, core_mask), (small, small))
    base_own = jnp.where(sec_pos % 2 == 0, swap(base_blocks), base_rows)
    base = lax.all_gather(base_own, "sec", axis=0)
    (sent,) = call(launch_kernel, (*scalars, angle_ids), (illum_amp, *tables), (blocks,))
    fields, screen = [], []
    for layer in range(3):
        kernel = functools.partial(forward_kernel, layer)
        sent, field_now, screen_now = call(kernel, scalars, (swap(sent), base, *tables), (blocks, saved, saved))
        fields.append(field_now)
        screen.append(screen_now)
    target = lax.dynamic_slice_in_dim(measured, sec_pos * SHARE, SHARE, 0)
    (sent,) = call(turn_kernel, scalars, (swap(sent), base, target, *tables), (wide_blocks,))
    third = swap(sent)
    kernel = functools.partial(adjoint_kernel, False)
    sent, second = call(
        kernel, scalars, (third, fields[2], screen[2], *tables), (blocks, (GROUPS, WIDE, LANES))
    )
    kernel = functools.partial(adjoint_kernel, True)
    (sent,) = call(kernel, scalars, (swap(sent), fields[1], screen[1], *tables), (wide_blocks,))
    (grads,) = call(
        last_kernel, scalars, (swap(sent), fields[0], third, second, *tables), ((4 * PEERS, 8, LANES),)
    )
    grads = lax.all_to_all(grads, ("sec", "row"), 0, 0, tiled=True)
    (result,) = call(sum_kernel, (), (grads,), ((1, WIDE, GRID),))
    return result


def solution(mesh):
    in_specs = (
        P("sec", "row", None),
        P("row", None),
        P("row", None),
        P(None, "row", None, None),
        P(),
        P(),
    )
    out_specs = P("sec", "row", None)
    return jax.shard_map(body, mesh=mesh, in_specs=in_specs, out_specs=out_specs, check_vma=False)
```

```python
import functools
import math

import jax
import jax.numpy as jnp
import numpy as np
from jax import lax
from jax.experimental import pallas as pl
from jax.experimental.pallas import tpu as pltpu
from jax.sharding import PartitionSpec as P

ratio_base = 0.75
ratio_step = 1.0 / 128.0
prop_scale = 150.0
core_step = 0.8
tilt_step = 8
angle_side = 8

LANES = 128
GROUPS = 8
GRID = GROUPS * LANES
WIDE = 32
PEERS = GRID // WIDE
SHARE = 2
FOLD = LANES // WIDE
CHUNK = 16
VMEM_LIMIT = 48 * 1024 * 1024


def dft_tables():
    counter = np.arange(LANES)
    angle = -2.0 * np.pi / LANES * (counter[:, None] * counter[None, :] % LANES)
    real, imag = np.cos(angle), np.sin(angle)
    full = np.block([[real, imag], [-imag, real]]).astype(np.float32)
    high = full.astype(jnp.bfloat16)
    low = (full - high.astype(np.float32)).astype(jnp.bfloat16)
    return high, low


def cos_sin(angle):
    turns = jnp.floor(angle * (2.0 / math.pi) + 0.5)
    rest = angle - turns * 1.5703125
    rest = rest - turns * 4.837512969970703e-4
    rest = rest - turns * 7.549789948768648e-8
    square = rest * rest
    sine = rest + rest * square * (
        -1.6666654611e-1 + square * (8.3321608736e-3 + square * -1.9515295891e-4)
    )
    cosine = (1.0 - 0.5 * square) + square * square * (
        4.166664568298827e-2 + square * (-1.388731625493765e-3 + square * 2.443315711809948e-5)
    )
    quarter = turns.astype(jnp.int32)
    swap = (quarter & 1) != 0
    cos_part = jnp.where(swap, sine, cosine)
    sin_part = jnp.where(swap, cosine, sine)
    cos_part = jnp.where(((quarter + 1) & 2) != 0, -cos_part, cos_part)
    sin_part = jnp.where((quarter & 2) != 0, -sin_part, sin_part)
    return cos_part, sin_part


def times(left, right):
    return (
        left[0] * right[0] - left[1] * right[1],
        left[0] * right[1] + left[1] * right[0],
    )


def times_conj(left, right):
    return (
        left[0] * right[0] + left[1] * right[1],
        left[1] * right[0] - left[0] * right[1],
    )


def plus(left, right):
    return (left[0] + right[0], left[1] + right[1])


def minus(left, right):
    return (left[0] - right[0], left[1] - right[1])


def quarter_turn(value, sign):
    if sign > 0:
        return (-value[1], value[0])
    return (value[1], -value[0])


def dft4(items, sign):
    even, odd = plus(items[0], items[2]), minus(items[0], items[2])
    other, rest = plus(items[1], items[3]), minus(items[1], items[3])
    rest = quarter_turn(rest, sign)
    return [plus(even, other), plus(odd, rest), minus(even, other), minus(odd, rest)]


def dft8(items, sign):
    even, odd = dft4(items[0::2], sign), dft4(items[1::2], sign)
    half = math.sqrt(0.5)
    first, third = odd[1], odd[3]
    if sign > 0:
        first = ((first[0] - first[1]) * half, (first[0] + first[1]) * half)
        third = ((-third[0] - third[1]) * half, (third[0] - third[1]) * half)
    else:
        first = ((first[0] + first[1]) * half, (first[1] - first[0]) * half)
        third = ((third[1] - third[0]) * half, (-third[0] - third[1]) * half)
    odd = [odd[0], first, quarter_turn(odd[2], sign), third]
    return [plus(e, o) for e, o in zip(even, odd)] + [minus(e, o) for e, o in zip(even, odd)]


def matmul_pair(left, right, high, low):
    both = jnp.concatenate([left, right], axis=1)
    upper = both.astype(jnp.bfloat16)
    lower = (both - upper.astype(jnp.float32)).astype(jnp.bfloat16)
    product = functools.partial(jnp.dot, preferred_element_type=jnp.float32)
    result = product(upper, high) + (product(lower, high) + product(upper, low))
    return result[:, :LANES], result[:, LANES:]


def filter_lines(wave, picks, twist, high, low, sign):
    rows = wave[0][0].shape[0]

    def stack(items, part):
        return jnp.concatenate([item[part] for item in items], axis=0)

    def pieces(real, imag):
        return [(real[k * rows : (k + 1) * rows], imag[k * rows : (k + 1) * rows]) for k in range(GROUPS)]

    parts = dft8(wave, -1)
    parts = [parts[0]] + [times(parts[k], twist[k]) for k in range(1, GROUPS)]
    spectrum = pieces(*matmul_pair(stack(parts, 0), stack(parts, 1), high, low))
    multiply = times if sign > 0 else times_conj
    spectrum = [multiply(value, pick) for value, pick in zip(spectrum, picks)]
    imag, real = matmul_pair(stack(spectrum, 1), stack(spectrum, 0), high, low)
    parts = pieces(real, imag)
    parts = [parts[0]] + [times_conj(parts[k], twist[k]) for k in range(1, GROUPS)]
    return dft8(parts, 1)


def line_filter(field, filters, twist, high, low, sign):
    result = []
    for wave, picks in zip(field, filters):
        chunks = []
        for first in range(0, WIDE, CHUNK):
            part = [(real[first : first + CHUNK], imag[first : first + CHUNK]) for real, imag in wave]
            chunks.append(filter_lines(part, picks, twist, high, low, sign))
        result.append(
            [
                tuple(jnp.concatenate([chunk[group][part] for chunk in chunks], axis=0) for part in range(2))
                for group in range(GROUPS)
            ]
        )
    return result


def exchange_blocks(items):
    lane = lax.broadcasted_iota(jnp.int32, items[0].shape, items[0].ndim - 1)
    axis = items[0].ndim - 1
    low_half, even = (lane & 64) == 0, (lane & 32) == 0
    halves = [None] * 4
    for i in range(2):
        halves[i] = jnp.where(low_half, items[i], pltpu.roll(items[i + 2], 64, axis))
        halves[i + 2] = jnp.where(low_half, pltpu.roll(items[i], 64, axis), items[i + 2])
    result = [None] * 4
    for i in (0, 2):
        result[i] = jnp.where(even, halves[i], pltpu.roll(halves[i + 1], 32, axis))
        result[i + 1] = jnp.where(even, pltpu.roll(halves[i], LANES - 32, axis), halves[i + 1])
    return result


def load_field(blocks_ref):
    turned = [
        jnp.concatenate([blocks_ref[GROUPS * i + j, :WIDE] for i in range(FOLD)], axis=0).T
        for j in range(GROUPS)
    ]
    field = [[[None, None] for _ in range(GROUPS)] for _ in range(SHARE)]
    for part in range(2):
        for wave in range(SHARE):
            first = (part * SHARE + wave) * WIDE
            for half in range(GROUPS // FOLD):
                rows = [turned[half * FOLD + i][first : first + WIDE] for i in range(FOLD)]
                points = jnp.concatenate(rows, axis=0).T
                for i in range(FOLD):
                    group = i * (GROUPS // FOLD) + half
                    field[wave][group][part] = points[i * WIDE : (i + 1) * WIDE]
    return field


def store_field(blocks_ref, field):
    for group in range(GROUPS):
        rows = [field[w][group][part] for part in range(2) for w in range(SHARE)]
        turned = jnp.concatenate(rows, axis=0).T
        for i in range(FOLD):
            blocks_ref[FOLD * group + i, :WIDE] = turned[i * WIDE : (i + 1) * WIDE]


def pack_plane(plane):
    blocks = []
    for group in range(GROUPS):
        rows = [plane[group]] + [pltpu.roll(plane[group], LANES - 8 * q, 1) for q in range(1, FOLD)]
        turned = jnp.concatenate(rows, axis=0).T
        blocks += [turned[i * WIDE : i * WIDE + 8] for i in range(FOLD)]
    return blocks


def unpack_plane(blocks):
    plane = []
    for group in range(GROUPS):
        items = exchange_blocks(blocks[FOLD * group : FOLD * (group + 1)])
        plane.append(jnp.concatenate(items, axis=0))
    return plane


def ratio_of(place_ref, wave):
    number = place_ref[2 + place_ref[0] * SHARE + wave]
    return ratio_base + ratio_step * number.astype(jnp.float32)


def filters_of(place_ref):
    row = lax.broadcasted_iota(jnp.int32, (GROUPS, LANES), 0)
    lane = lax.broadcasted_iota(jnp.int32, (GROUPS, LANES), 1)
    natural = row + GROUPS * lane
    signed = jnp.where(natural < GRID // 2, natural, natural - GRID)
    scaled = signed.astype(jnp.float32) * (2.0 / GRID)
    squares = scaled * scaled
    filters = []
    for wave in range(SHARE):
        real, imag = cos_sin((-prop_scale * ratio_of(place_ref, wave)) * squares)
        real, imag = real * (1.0 / GRID), imag * (1.0 / GRID)
        filters.append([(real[k : k + 1], imag[k : k + 1]) for k in range(GROUPS)])
    return filters


def twists():
    row = lax.broadcasted_iota(jnp.int32, (GROUPS, LANES), 0)
    lane = lax.broadcasted_iota(jnp.int32, (GROUPS, LANES), 1)
    real, imag = cos_sin((-2.0 * math.pi / GRID) * (row * lane).astype(jnp.float32))
    return [(real[k : k + 1], imag[k : k + 1]) for k in range(GROUPS)]


def inverse_ratio(place_ref, wave):
    ratio = ratio_of(place_ref, wave)
    return 1.0 / jnp.full((8, LANES), ratio, jnp.float32)[:1]


def copies(pairs, sems):
    return [pltpu.make_async_copy(source, target, sems.at[i]) for i, (source, target) in enumerate(pairs)]


def start(moves):
    for move in moves:
        move.start()


def wait(moves):
    for move in moves:
        move.wait()


def launch_kernel(
    waves,
    place_ref,
    illum_hbm,
    high_hbm,
    low_hbm,
    measured_hbm,
    out_ref,
    target_ref,
    illum_ref,
    high_ref,
    low_ref,
    measured_ref,
    sems,
):
    own = measured_hbm.at[pl.ds(place_ref[0] * SHARE, SHARE)]
    moves = copies(
        [(illum_hbm, illum_ref), (high_hbm, high_ref), (low_hbm, low_ref), (own, measured_ref)], sems
    )
    start(moves)
    twist = twists()
    filters = filters_of(place_ref)
    tilted = []
    for wave in range(SHARE):
        pick = place_ref[2 + waves + place_ref[0] * SHARE + wave]
        tilt_x = ((pick & (angle_side - 1)) - angle_side // 2) * tilt_step
        tilt_y = ((pick >> 3) - angle_side // 2) * tilt_step
        row = lax.broadcasted_iota(jnp.int32, (WIDE, LANES), 0) + place_ref[1] * WIDE

        def wheel(product):
            turned = ((product + GRID // 2) & (GRID - 1)) - GRID // 2
            return cos_sin((2.0 * math.pi / GRID) * turned.astype(jnp.float32))

        down = wheel(tilt_y * row)
        groups = []
        for group in range(GROUPS):
            column = lax.broadcasted_iota(jnp.int32, (8, LANES), 1) + group * LANES
            across = wheel(tilt_x * column)
            groups.append(times(down, (across[0][:1], across[1][:1])))
        tilted.append(groups)
    wait(moves[:3])
    field = []
    for wave in range(SHARE):
        groups = []
        for group in range(GROUPS):
            bright = illum_ref[:, group * LANES : (group + 1) * LANES]
            groups.append((bright * tilted[wave][group][0], bright * tilted[wave][group][1]))
        field.append(groups)
    field = line_filter(field, filters, twist, high_ref[...], low_ref[...], 1)
    store_field(out_ref, field)
    wait(moves[3:])
    for wave in range(SHARE):
        for part in range(2):
            target_ref[wave, part] = measured_ref[wave, :, part]


def save(kept_ref, field):
    for wave in range(SHARE):
        for group in range(GROUPS):
            for part in range(2):
                kept_ref[wave, group, part] = field[wave][group][part]


def kept(kept_ref):
    return [
        [(kept_ref[wave, group, 0], kept_ref[wave, group, 1]) for group in range(GROUPS)]
        for wave in range(SHARE)
    ]


def read_base(base_refs, layer, place_ref):
    slot = (place_ref[0] - layer) & 3

    def block(index):
        value = base_refs[0][index]
        for shift in range(1, len(base_refs)):
            value = jnp.where(slot == shift, base_refs[shift][index], value)
        return value

    if layer % 2:
        return [
            jnp.concatenate([block(tile * GROUPS + group) for tile in range(FOLD)], axis=0)
            for group in range(GROUPS)
        ]
    return unpack_plane([block(peer) for peer in range(PEERS)])


def screens(base_refs, layer, place_ref):
    base = read_base(base_refs, layer, place_ref)
    result = []
    for wave in range(SHARE):
        scale = inverse_ratio(place_ref, wave)
        result.append([cos_sin(base[group] * scale) for group in range(GROUPS)])
    return result


def gradient(adjoint, field, place_ref):
    total = [None] * GROUPS
    for wave in range(SHARE):
        scale = inverse_ratio(place_ref, wave)
        for group in range(GROUPS):
            left, right = adjoint[wave][group], field[wave][group]
            term = (left[1] * right[0] - left[0] * right[1]) * scale
            total[group] = term if wave == 0 else total[group] + term
    return total


def each(function, left, right):
    return [[function(a, b) for a, b in zip(p, q)] for p, q in zip(left, right)]


def forward_kernel(
    layer, place_ref, in_ref, high_ref, low_ref, base_0, base_1, base_2, base_3, out_ref, field_ref, *screen_ref
):
    high, low, twist = high_ref[...], low_ref[...], twists()
    filters = filters_of(place_ref)
    field = line_filter(load_field(in_ref), filters, twist, high, low, 1)
    screen = screens((base_0, base_1, base_2, base_3), layer, place_ref)
    if layer:
        save(screen_ref[0], screen)
    field = each(times, field, screen)
    save(field_ref, field)
    store_field(out_ref, line_filter(field, filters, twist, high, low, 1))


def turn_kernel(
    place_ref, in_ref, high_ref, low_ref, base_0, base_1, base_2, base_3, target_ref, out_ref
):
    high, low, twist = high_ref[...], low_ref[...], twists()
    filters = filters_of(place_ref)
    field = line_filter(load_field(in_ref), filters, twist, high, low, 1)
    screen = screens((base_0, base_1, base_2, base_3), 3, place_ref)
    field = each(times, field, screen)
    adjoint = []
    for wave in range(SHARE):
        groups = []
        for group in range(GROUPS):
            lanes = slice(group * LANES, (group + 1) * LANES)
            goal = (target_ref[wave, 0, :, lanes], target_ref[wave, 1, :, lanes])
            groups.append(minus(field[wave][group], goal))
        adjoint.append(groups)
    blocks = pack_plane(gradient(adjoint, field, place_ref))
    for peer in range(PEERS):
        out_ref[peer, WIDE:] = blocks[peer]
    adjoint = each(times_conj, adjoint, screen)
    store_field(out_ref, line_filter(adjoint, filters, twist, high, low, -1))


def adjoint_kernel(
    with_plane, place_ref, in_ref, high_ref, low_ref, field_ref, screen_ref, out_ref, *grad_ref
):
    high, low, twist = high_ref[...], low_ref[...], twists()
    filters = filters_of(place_ref)
    adjoint = line_filter(load_field(in_ref), filters, twist, high, low, -1)
    grad = gradient(adjoint, kept(field_ref), place_ref)
    if with_plane:
        blocks = pack_plane(grad)
        for peer in range(PEERS):
            out_ref[peer, WIDE:] = blocks[peer]
    else:
        for group in range(GROUPS):
            grad_ref[0][group] = grad[group]
    adjoint = each(times_conj, adjoint, kept(screen_ref))
    store_field(out_ref, line_filter(adjoint, filters, twist, high, low, -1))


def last_kernel(place_ref, in_ref, high_ref, low_ref, third_ref, second_ref, field_ref, out_ref):
    high, low, twist = high_ref[...], low_ref[...], twists()
    filters = filters_of(place_ref)
    adjoint = line_filter(load_field(in_ref), filters, twist, high, low, -1)
    planes = [
        gradient(adjoint, kept(field_ref), place_ref),
        unpack_plane([in_ref[peer, WIDE:] for peer in range(PEERS)]),
        [second_ref[group] for group in range(GROUPS)],
        unpack_plane([third_ref[peer, WIDE:] for peer in range(PEERS)]),
    ]
    for group in range(GROUPS):
        turned = jnp.concatenate([plane[group] for plane in planes], axis=0).T
        for i in range(FOLD):
            rows = [turned[i * WIDE + 8 * q : i * WIDE + 8 * (q + 1)] for q in range(FOLD)]
            for layer, block in enumerate(exchange_blocks(rows)):
                out_ref[layer * PEERS + group * FOLD + i] = block


def sum_kernel(in_ref, out_ref):
    total = [
        (in_ref[peer] + in_ref[PEERS + peer]) + (in_ref[2 * PEERS + peer] + in_ref[3 * PEERS + peer])
        for peer in range(PEERS)
    ]
    plane = unpack_plane(total)
    for group in range(GROUPS):
        out_ref[0, :, group * LANES : (group + 1) * LANES] = plane[group]


def base_kernel(slice_hbm, mask_hbm, rows_ref, out_ref, slice_ref, mask_ref, sems):
    moves = copies([(slice_hbm, slice_ref), (mask_hbm, mask_ref)], sems)
    start(moves)
    wait(moves)
    base = []
    for group in range(GROUPS):
        lanes = slice(group * LANES, (group + 1) * LANES)
        plane = core_step * mask_ref[:, lanes].astype(jnp.float32) + slice_ref[0, :, lanes]
        base.append(plane)
        for tile in range(FOLD):
            rows_ref[tile * GROUPS + group] = plane[tile * 8 : (tile + 1) * 8]
    blocks = pack_plane(base)
    for peer in range(PEERS):
        out_ref[peer] = blocks[peer]


def call(kernel, scalars, near, far, outs, scratch=(), moves=1):
    specs = [pl.BlockSpec(memory_space=pltpu.SMEM)] * len(scalars)
    specs += [pl.BlockSpec(memory_space=pltpu.VMEM)] * len(near)
    specs += [pl.BlockSpec(memory_space=pltpu.HBM)] * len(far)
    scratch = [pltpu.VMEM(shape, dtype) for shape, dtype in scratch]
    if scratch:
        scratch.append(pltpu.SemaphoreType.DMA((moves,)))
    return pl.pallas_call(
        kernel,
        out_shape=[place(shape, jnp.float32) for shape, place in outs],
        in_specs=specs,
        out_specs=[pl.BlockSpec(memory_space=pltpu.VMEM)] * len(outs),
        scratch_shapes=scratch,
        compiler_params=pltpu.CompilerParams(vmem_limit_bytes=VMEM_LIMIT),
    )(*scalars, *near, *far)


def near(shape):
    return (shape, pltpu.VMEM)


def free(shape):
    return (shape, jax.ShapeDtypeStruct)


def in_hbm(*arrays):
    return tuple(pltpu.with_memory_space_constraint(array, pltpu.HBM) for array in arrays)


def body(index_slices, core_mask, illum_amp, measured, wave_ids, angle_ids):
    row_pos, sec_pos = lax.axis_index("row"), lax.axis_index("sec")
    sec_count, waves = lax.axis_size("sec"), wave_ids.shape[0]
    tables = tuple(jnp.asarray(table) for table in dft_tables())
    place = jnp.concatenate([sec_pos[None], row_pos[None], wave_ids, angle_ids]).astype(jnp.int32)
    swap = functools.partial(lax.all_to_all, axis_name="row", split_axis=0, concat_axis=0, tiled=True)
    blocks, small = (PEERS, WIDE, LANES), (PEERS, 8, LANES)
    wide_blocks = (PEERS, WIDE + 8, LANES)
    saved = (SHARE, GROUPS, 2, WIDE, LANES)
    table = ((2 * LANES, 2 * LANES), jnp.bfloat16)
    base_rows, base_blocks = call(
        base_kernel,
        (),
        (),
        in_hbm(index_slices, core_mask),
        (free(small), free(small)),
        scratch=((index_slices.shape, jnp.float32), (core_mask.shape, jnp.int32)),
        moves=2,
    )
    sent, target = call(
        functools.partial(launch_kernel, waves),
        (place,),
        (),
        in_hbm(illum_amp, *tables, measured),
        (free(blocks), near((SHARE, 2, WIDE, GRID))),
        scratch=(
            (illum_amp.shape, jnp.float32),
            table,
            table,
            ((SHARE, *measured.shape[1:]), jnp.float32),
        ),
        moves=4,
    )
    base_own = jnp.where(sec_pos % 2 == 0, swap(base_blocks), base_rows)
    base = [base_own]
    for shift in range(1, sec_count):
        base.append(lax.ppermute(base_own, "sec", [(i, (i + shift) % sec_count) for i in range(sec_count)]))
    fields, screen = [], []
    for layer in range(3):
        sent, field_now, *screen_now = call(
            functools.partial(forward_kernel, layer),
            (place,),
            (swap(sent), *tables, *base),
            (),
            (free(blocks),) + (near(saved),) * (2 if layer else 1),
        )
        fields.append(field_now)
        screen += screen_now
    (sent,) = call(
        turn_kernel,
        (place,),
        (swap(sent), *tables, *base, target),
        (),
        (free(wide_blocks),),
    )
    third = swap(sent)
    sent, second = call(
        functools.partial(adjoint_kernel, False),
        (place,),
        (third, *tables, fields[2], screen[1]),
        (),
        (free(blocks), near((GROUPS, WIDE, LANES))),
    )
    (sent,) = call(
        functools.partial(adjoint_kernel, True),
        (place,),
        (swap(sent), *tables, fields[1], screen[0]),
        (),
        (free(wide_blocks),),
    )
    (grads,) = call(
        last_kernel,
        (place,),
        (swap(sent), *tables, third, second, fields[0]),
        (),
        (free((4 * PEERS, 8, LANES)),),
    )
    grads = lax.all_to_all(grads, ("sec", "row"), 0, 0, tiled=True)
    (result,) = call(sum_kernel, (), (grads,), (), (free((1, WIDE, GRID)),))
    return result


def solution(mesh):
    in_specs = (
        P("sec", "row", None),
        P("row", None),
        P("row", None),
        P(None, "row", None, None),
        P(),
        P(),
    )
    out_specs = P("sec", "row", None)
    return jax.shard_map(body, mesh=mesh, in_specs=in_specs, out_specs=out_specs, check_vma=False)
```

```python
import functools
import math

import jax
import jax.numpy as jnp
import numpy as np
from jax import lax
from jax.experimental import pallas as pl
from jax.experimental.pallas import tpu as pltpu
from jax.sharding import PartitionSpec as P

ratio_base = 0.75
ratio_step = 1.0 / 128.0
prop_scale = 150.0
core_step = 0.8
tilt_step = 8
angle_side = 8

LANES = 128
GROUPS = 8
GRID = GROUPS * LANES
WIDE = 32
PEERS = GRID // WIDE
SHARE = 2
FOLD = LANES // WIDE
CHUNK = 16
VMEM_LIMIT = 48 * 1024 * 1024


def dft_tables():
    counter = np.arange(LANES)
    angle = -2.0 * np.pi / LANES * (counter[:, None] * counter[None, :] % LANES)
    real, imag = np.cos(angle), np.sin(angle)
    full = np.block([[real, imag], [-imag, real]]).astype(np.float32)
    high = full.astype(jnp.bfloat16)
    low = (full - high.astype(np.float32)).astype(jnp.bfloat16)
    return high, low


def cos_sin(angle):
    turns = jnp.floor(angle * (2.0 / math.pi) + 0.5)
    rest = angle - turns * 1.5703125
    rest = rest - turns * 4.837512969970703e-4
    rest = rest - turns * 7.549789948768648e-8
    square = rest * rest
    sine = rest + rest * square * (
        -1.6666654611e-1 + square * (8.3321608736e-3 + square * -1.9515295891e-4)
    )
    cosine = (1.0 - 0.5 * square) + square * square * (
        4.166664568298827e-2 + square * (-1.388731625493765e-3 + square * 2.443315711809948e-5)
    )
    quarter = turns.astype(jnp.int32)
    swap = (quarter & 1) != 0
    cos_part = jnp.where(swap, sine, cosine)
    sin_part = jnp.where(swap, cosine, sine)
    cos_part = jnp.where(((quarter + 1) & 2) != 0, -cos_part, cos_part)
    sin_part = jnp.where((quarter & 2) != 0, -sin_part, sin_part)
    return cos_part, sin_part


def times(left, right):
    return (
        left[0] * right[0] - left[1] * right[1],
        left[0] * right[1] + left[1] * right[0],
    )


def times_conj(left, right):
    return (
        left[0] * right[0] + left[1] * right[1],
        left[1] * right[0] - left[0] * right[1],
    )


def plus(left, right):
    return (left[0] + right[0], left[1] + right[1])


def minus(left, right):
    return (left[0] - right[0], left[1] - right[1])


def quarter_turn(value, sign):
    if sign > 0:
        return (-value[1], value[0])
    return (value[1], -value[0])


def dft4(items, sign):
    even, odd = plus(items[0], items[2]), minus(items[0], items[2])
    other, rest = plus(items[1], items[3]), minus(items[1], items[3])
    rest = quarter_turn(rest, sign)
    return [plus(even, other), plus(odd, rest), minus(even, other), minus(odd, rest)]


def dft8(items, sign):
    even, odd = dft4(items[0::2], sign), dft4(items[1::2], sign)
    half = math.sqrt(0.5)
    first, third = odd[1], odd[3]
    if sign > 0:
        first = ((first[0] - first[1]) * half, (first[0] + first[1]) * half)
        third = ((-third[0] - third[1]) * half, (third[0] - third[1]) * half)
    else:
        first = ((first[0] + first[1]) * half, (first[1] - first[0]) * half)
        third = ((third[1] - third[0]) * half, (-third[0] - third[1]) * half)
    odd = [odd[0], first, quarter_turn(odd[2], sign), third]
    return [plus(e, o) for e, o in zip(even, odd)] + [minus(e, o) for e, o in zip(even, odd)]


def matmul_pair(left, right, high, low):
    both = jnp.concatenate([left, right], axis=1)
    upper = both.astype(jnp.bfloat16)
    lower = (both - upper.astype(jnp.float32)).astype(jnp.bfloat16)
    product = functools.partial(jnp.dot, preferred_element_type=jnp.float32)
    result = product(upper, high) + (product(lower, high) + product(upper, low))
    return result[:, :LANES], result[:, LANES:]


def filter_lines(wave, picks, twist, high, low, sign):
    rows = wave[0][0].shape[0]

    def stack(items, part):
        return jnp.concatenate([item[part] for item in items], axis=0)

    def pieces(real, imag):
        return [(real[k * rows : (k + 1) * rows], imag[k * rows : (k + 1) * rows]) for k in range(GROUPS)]

    parts = dft8(wave, -1)
    parts = [parts[0]] + [times(parts[k], twist[k]) for k in range(1, GROUPS)]
    spectrum = pieces(*matmul_pair(stack(parts, 0), stack(parts, 1), high, low))
    multiply = times if sign > 0 else times_conj
    spectrum = [multiply(value, pick) for value, pick in zip(spectrum, picks)]
    imag, real = matmul_pair(stack(spectrum, 1), stack(spectrum, 0), high, low)
    parts = pieces(real, imag)
    parts = [parts[0]] + [times_conj(parts[k], twist[k]) for k in range(1, GROUPS)]
    return dft8(parts, 1)


def line_filter(field, filters, twist, high, low, sign):
    result = []
    for wave, picks in zip(field, filters):
        chunks = []
        for first in range(0, WIDE, CHUNK):
            part = [(real[first : first + CHUNK], imag[first : first + CHUNK]) for real, imag in wave]
            chunks.append(filter_lines(part, picks, twist, high, low, sign))
        result.append(
            [
                tuple(jnp.concatenate([chunk[group][part] for chunk in chunks], axis=0) for part in range(2))
                for group in range(GROUPS)
            ]
        )
    return result


def exchange_blocks(items):
    lane = lax.broadcasted_iota(jnp.int32, items[0].shape, items[0].ndim - 1)
    axis = items[0].ndim - 1
    low_half, even = (lane & 64) == 0, (lane & 32) == 0
    halves = [None] * 4
    for i in range(2):
        halves[i] = jnp.where(low_half, items[i], pltpu.roll(items[i + 2], 64, axis))
        halves[i + 2] = jnp.where(low_half, pltpu.roll(items[i], 64, axis), items[i + 2])
    result = [None] * 4
    for i in (0, 2):
        result[i] = jnp.where(even, halves[i], pltpu.roll(halves[i + 1], 32, axis))
        result[i + 1] = jnp.where(even, pltpu.roll(halves[i], LANES - 32, axis), halves[i + 1])
    return result


def load_field(blocks_ref, start):
    turned = [
        jnp.concatenate([blocks_ref[GROUPS * i + j, start : start + WIDE] for i in range(FOLD)], axis=0).T
        for j in range(GROUPS)
    ]
    field = [[[None, None] for _ in range(GROUPS)] for _ in range(SHARE)]
    for part in range(2):
        for wave in range(SHARE):
            first = (part * SHARE + wave) * WIDE
            for half in range(GROUPS // FOLD):
                rows = [turned[half * FOLD + i][first : first + WIDE] for i in range(FOLD)]
                points = jnp.concatenate(rows, axis=0).T
                for i in range(FOLD):
                    group = i * (GROUPS // FOLD) + half
                    field[wave][group][part] = points[i * WIDE : (i + 1) * WIDE]
    return field


def store_field(blocks_ref, start, field):
    for group in range(GROUPS):
        rows = [field[w][group][part] for part in range(2) for w in range(SHARE)]
        turned = jnp.concatenate(rows, axis=0).T
        for i in range(FOLD):
            blocks_ref[FOLD * group + i, start : start + WIDE] = turned[i * WIDE : (i + 1) * WIDE]


def pack_plane(plane):
    blocks = []
    for group in range(GROUPS):
        rows = [plane[group]] + [pltpu.roll(plane[group], LANES - 8 * q, 1) for q in range(1, FOLD)]
        turned = jnp.concatenate(rows, axis=0).T
        blocks += [turned[i * WIDE : i * WIDE + 8] for i in range(FOLD)]
    return blocks


def store_plane(blocks_ref, start, plane):
    blocks = pack_plane(plane)
    for peer in range(PEERS):
        blocks_ref[peer, start : start + 8] = blocks[peer]


def load_plane(blocks_ref, start):
    return unpack_plane([blocks_ref[peer, start : start + 8] for peer in range(PEERS)])


def unpack_plane(blocks):
    plane = []
    for group in range(GROUPS):
        items = exchange_blocks(blocks[FOLD * group : FOLD * (group + 1)])
        plane.append(jnp.concatenate(items, axis=0))
    return plane


def ratio_of(place_ref, wave):
    number = place_ref[2 + place_ref[0] * SHARE + wave]
    return ratio_base + ratio_step * number.astype(jnp.float32)


def filters_of(place_ref):
    row = lax.broadcasted_iota(jnp.int32, (GROUPS, LANES), 0)
    lane = lax.broadcasted_iota(jnp.int32, (GROUPS, LANES), 1)
    natural = row + GROUPS * lane
    signed = jnp.where(natural < GRID // 2, natural, natural - GRID)
    scaled = signed.astype(jnp.float32) * (2.0 / GRID)
    squares = scaled * scaled
    filters = []
    for wave in range(SHARE):
        real, imag = cos_sin((-prop_scale * ratio_of(place_ref, wave)) * squares)
        real, imag = real * (1.0 / GRID), imag * (1.0 / GRID)
        filters.append([(real[k : k + 1], imag[k : k + 1]) for k in range(GROUPS)])
    return filters


def twists():
    row = lax.broadcasted_iota(jnp.int32, (GROUPS, LANES), 0)
    lane = lax.broadcasted_iota(jnp.int32, (GROUPS, LANES), 1)
    real, imag = cos_sin((-2.0 * math.pi / GRID) * (row * lane).astype(jnp.float32))
    return [(real[k : k + 1], imag[k : k + 1]) for k in range(GROUPS)]


def inverse_ratio(place_ref, wave):
    ratio = ratio_of(place_ref, wave)
    return 1.0 / jnp.full((8, LANES), ratio, jnp.float32)[:1]


def copies(pairs, sems):
    return [pltpu.make_async_copy(source, target, sems.at[i]) for i, (source, target) in enumerate(pairs)]


def start(moves):
    for move in moves:
        move.start()


def wait(moves):
    for move in moves:
        move.wait()


def launch_kernel(
    waves,
    place_ref,
    illum_hbm,
    high_hbm,
    low_hbm,
    measured_hbm,
    out_ref,
    target_ref,
    illum_ref,
    high_ref,
    low_ref,
    measured_ref,
    sems,
):
    own = measured_hbm.at[pl.ds(place_ref[0] * SHARE, SHARE)]
    moves = copies(
        [(illum_hbm, illum_ref), (high_hbm, high_ref), (low_hbm, low_ref), (own, measured_ref)], sems
    )
    start(moves)
    twist = twists()
    filters = filters_of(place_ref)
    tilted = []
    for wave in range(SHARE):
        pick = place_ref[2 + waves + place_ref[0] * SHARE + wave]
        tilt_x = ((pick & (angle_side - 1)) - angle_side // 2) * tilt_step
        tilt_y = ((pick >> 3) - angle_side // 2) * tilt_step
        row = lax.broadcasted_iota(jnp.int32, (WIDE, LANES), 0) + place_ref[1] * WIDE

        def wheel(product):
            turned = ((product + GRID // 2) & (GRID - 1)) - GRID // 2
            return cos_sin((2.0 * math.pi / GRID) * turned.astype(jnp.float32))

        down = wheel(tilt_y * row)
        groups = []
        for group in range(GROUPS):
            column = lax.broadcasted_iota(jnp.int32, (8, LANES), 1) + group * LANES
            across = wheel(tilt_x * column)
            groups.append(times(down, (across[0][:1], across[1][:1])))
        tilted.append(groups)
    wait(moves[:3])
    field = []
    for wave in range(SHARE):
        groups = []
        for group in range(GROUPS):
            bright = illum_ref[:, group * LANES : (group + 1) * LANES]
            groups.append((bright * tilted[wave][group][0], bright * tilted[wave][group][1]))
        field.append(groups)
    field = line_filter(field, filters, twist, high_ref[...], low_ref[...], 1)
    store_field(out_ref, 0, field)
    wait(moves[3:])
    for wave in range(SHARE):
        for part in range(2):
            target_ref[wave, part] = measured_ref[wave, :, part]


def save(kept_ref, field):
    for wave in range(SHARE):
        for group in range(GROUPS):
            for part in range(2):
                kept_ref[wave, group, part] = field[wave][group][part]


def kept(kept_ref):
    return [
        [(kept_ref[wave, group, 0], kept_ref[wave, group, 1]) for group in range(GROUPS)]
        for wave in range(SHARE)
    ]


def screens(base, place_ref):
    result = []
    for wave in range(SHARE):
        scale = inverse_ratio(place_ref, wave)
        result.append([cos_sin(plane * scale) for plane in base])
    return result


def gradient(target, field, place_ref):
    total = [None] * GROUPS
    for wave in range(SHARE):
        scale = inverse_ratio(place_ref, wave)
        for group in range(GROUPS):
            left, right = target[wave][group], field[wave][group]
            term = (left[0] * right[1] - left[1] * right[0]) * scale
            total[group] = term if wave == 0 else total[group] + term
    return total


def lanes_of(group):
    return slice(group * LANES, (group + 1) * LANES)


def planes_of(ref):
    return [ref[:, lanes_of(group)] for group in range(GROUPS)]


def target_of(target_ref):
    return [
        [(target_ref[wave, 0, :, lanes_of(group)], target_ref[wave, 1, :, lanes_of(group)]) for group in range(GROUPS)]
        for wave in range(SHARE)
    ]


def each(function, left, right):
    return [[function(a, b) for a, b in zip(p, q)] for p, q in zip(left, right)]


def begin_kernel(
    place_ref, launched_ref, slices_ref, mask_ref, target_ref, high_ref, low_ref, out_ref, base_ref, screen_ref
):
    high, low, twist = high_ref[...], low_ref[...], twists()
    filters = filters_of(place_ref)
    mask = [core_step * mask_ref[:, lanes_of(group)].astype(jnp.float32) for group in range(GROUPS)]

    def base_of(layer):
        return [mask[group] + slices_ref[layer, :, lanes_of(group)] for group in range(GROUPS)]

    for peer in range(PEERS):
        out_ref[peer, :WIDE] = launched_ref[peer]
    store_plane(out_ref, 2 * WIDE, base_of(0))
    store_plane(out_ref, 2 * WIDE + 8, base_of(2))
    for group, plane in enumerate(base_of(1)):
        base_ref[:, lanes_of(group)] = plane
    screen = screens(base_of(3), place_ref)
    save(screen_ref, screen)
    target = each(times_conj, target_of(target_ref), screen)
    store_field(out_ref, WIDE, line_filter(target, filters, twist, high, low, -1))


def first_kernel(place_ref, in_ref, high_ref, low_ref, out_ref, field_ref, target_ref, screen_ref):
    high, low, twist = high_ref[...], low_ref[...], twists()
    filters = filters_of(place_ref)
    field = line_filter(load_field(in_ref, 0), filters, twist, high, low, 1)
    field = each(times, field, screens(load_plane(in_ref, 2 * WIDE), place_ref))
    save(field_ref, field)
    store_field(out_ref, 0, line_filter(field, filters, twist, high, low, 1))
    target = line_filter(load_field(in_ref, WIDE), filters, twist, high, low, -1)
    save(target_ref, target)
    screen = screens(load_plane(in_ref, 2 * WIDE + 8), place_ref)
    save(screen_ref, screen)
    target = each(times_conj, target, screen)
    store_field(out_ref, WIDE, line_filter(target, filters, twist, high, low, -1))


def second_kernel(place_ref, in_ref, high_ref, low_ref, base_ref, out_ref, grad_ref):
    high, low, twist = high_ref[...], low_ref[...], twists()
    filters = filters_of(place_ref)
    screen = screens(planes_of(base_ref), place_ref)
    field = line_filter(load_field(in_ref, 0), filters, twist, high, low, 1)
    field = each(times, field, screen)
    target = line_filter(load_field(in_ref, WIDE), filters, twist, high, low, -1)
    for group, plane in enumerate(gradient(target, field, place_ref)):
        grad_ref[:, lanes_of(group)] = plane
    store_field(out_ref, 0, line_filter(field, filters, twist, high, low, 1))
    target = each(times_conj, target, screen)
    store_field(out_ref, WIDE, line_filter(target, filters, twist, high, low, -1))


def third_kernel(place_ref, in_ref, high_ref, low_ref, field_ref, target_ref, screen_ref, out_ref):
    high, low, twist = high_ref[...], low_ref[...], twists()
    filters = filters_of(place_ref)
    field = line_filter(load_field(in_ref, 0), filters, twist, high, low, 1)
    field = each(times, field, kept(screen_ref))
    store_plane(out_ref, WIDE + 8, gradient(kept(target_ref), field, place_ref))
    store_field(out_ref, 0, line_filter(field, filters, twist, high, low, 1))
    target = line_filter(load_field(in_ref, WIDE), filters, twist, high, low, -1)
    store_plane(out_ref, WIDE, gradient(target, kept(field_ref), place_ref))


def last_kernel(place_ref, in_ref, high_ref, low_ref, screen_ref, target_ref, first_ref, out_ref):
    high, low, twist = high_ref[...], low_ref[...], twists()
    filters = filters_of(place_ref)
    field = line_filter(load_field(in_ref, 0), filters, twist, high, low, 1)
    field = each(times, field, kept(screen_ref))
    planes = [
        load_plane(in_ref, WIDE),
        planes_of(first_ref),
        load_plane(in_ref, WIDE + 8),
        gradient(target_of(target_ref), field, place_ref),
    ]
    for layer, plane in enumerate(planes):
        for group in range(GROUPS):
            out_ref[layer, :, lanes_of(group)] = plane[group]


def sum_kernel(in_ref, out_ref):
    total = in_ref[0]
    for section in range(1, in_ref.shape[0]):
        total = total + in_ref[section]
    out_ref[0] = total


def call(kernel, scalars, near, far, outs, scratch=(), moves=1):
    specs = [pl.BlockSpec(memory_space=pltpu.SMEM)] * len(scalars)
    specs += [pl.BlockSpec(memory_space=pltpu.VMEM)] * len(near)
    specs += [pl.BlockSpec(memory_space=pltpu.HBM)] * len(far)
    scratch = [pltpu.VMEM(shape, dtype) for shape, dtype in scratch]
    if scratch:
        scratch.append(pltpu.SemaphoreType.DMA((moves,)))
    return pl.pallas_call(
        kernel,
        out_shape=[place(shape, jnp.float32) for shape, place in outs],
        in_specs=specs,
        out_specs=[pl.BlockSpec(memory_space=pltpu.VMEM)] * len(outs),
        scratch_shapes=scratch,
        compiler_params=pltpu.CompilerParams(vmem_limit_bytes=VMEM_LIMIT),
    )(*scalars, *near, *far)


def near(shape):
    return (shape, pltpu.VMEM)


def free(shape):
    return (shape, jax.ShapeDtypeStruct)


def in_hbm(*arrays):
    return tuple(pltpu.with_memory_space_constraint(array, pltpu.HBM) for array in arrays)


def body(index_slices, core_mask, illum_amp, measured, wave_ids, angle_ids):
    row_pos, sec_pos = lax.axis_index("row"), lax.axis_index("sec")
    sec_count, waves = lax.axis_size("sec"), wave_ids.shape[0]
    tables = tuple(jnp.asarray(table) for table in dft_tables())
    place = jnp.concatenate([sec_pos[None], row_pos[None], wave_ids, angle_ids]).astype(jnp.int32)
    swap = functools.partial(lax.all_to_all, split_axis=0, concat_axis=0, tiled=True)
    plane, saved = (WIDE, GRID), (SHARE, GROUPS, 2, WIDE, LANES)
    table = ((2 * LANES, 2 * LANES), jnp.bfloat16)

    def blocks(rows):
        return free((PEERS, rows, LANES))

    slices = swap(jnp.broadcast_to(index_slices, (sec_count, *plane)), "sec")
    launched, target = call(
        functools.partial(launch_kernel, waves),
        (place,),
        (),
        in_hbm(illum_amp, *tables, measured),
        (near((PEERS, WIDE, LANES)), near((SHARE, 2, *plane))),
        scratch=((plane, jnp.float32), table, table, ((SHARE, *measured.shape[1:]), jnp.float32)),
        moves=4,
    )
    sent, base, screen_3 = call(
        begin_kernel,
        (place,),
        (launched, slices, core_mask, target, *tables),
        (),
        (blocks(2 * WIDE + 16), near(plane), near(saved)),
    )
    sent, field_0, target_2, screen_2 = call(
        first_kernel, (place,), (swap(sent, "row"), *tables), (), (blocks(2 * WIDE),) + (near(saved),) * 3
    )
    sent, grad_1 = call(
        second_kernel, (place,), (swap(sent, "row"), *tables, base), (), (blocks(2 * WIDE), near(plane))
    )
    (sent,) = call(
        third_kernel,
        (place,),
        (swap(sent, "row"), *tables, field_0, target_2, screen_2),
        (),
        (blocks(WIDE + 16),),
    )
    (grads,) = call(
        last_kernel,
        (place,),
        (swap(sent, "row"), *tables, screen_3, target, grad_1),
        (),
        (free((sec_count, *plane)),),
    )
    (result,) = call(sum_kernel, (), (swap(grads, "sec"),), (), (free((1, *plane)),))
    return result


def solution(mesh):
    in_specs = (
        P("sec", "row", None),
        P("row", None),
        P("row", None),
        P(None, "row", None, None),
        P(),
        P(),
    )
    out_specs = P("sec", "row", None)
    return jax.shard_map(body, mesh=mesh, in_specs=in_specs, out_specs=out_specs, check_vma=False)
```

```python
import functools
import math

import jax
import jax.numpy as jnp
import numpy as np
from jax import lax
from jax.experimental import pallas as pl
from jax.experimental.pallas import tpu as pltpu
from jax.sharding import PartitionSpec as P

ratio_base = 0.75
ratio_step = 1.0 / 128.0
prop_scale = 150.0
core_step = 0.8
tilt_step = 8
angle_side = 8

LANES = 128
GROUPS = 8
GRID = GROUPS * LANES
WIDE = 32
PEERS = GRID // WIDE
SHARE = 2
FOLD = LANES // WIDE
CHUNK = 16
VMEM_LIMIT = 48 * 1024 * 1024


def dft_tables():
    counter = np.arange(LANES)
    angle = -2.0 * np.pi / LANES * (counter[:, None] * counter[None, :] % LANES)
    real, imag = np.cos(angle), np.sin(angle)
    full = np.block([[real, imag], [-imag, real]]).astype(np.float32)
    high = full.astype(jnp.bfloat16)
    low = (full - high.astype(np.float32)).astype(jnp.bfloat16)
    return high, low


def cos_sin(angle):
    turns = jnp.floor(angle * (2.0 / math.pi) + 0.5)
    rest = angle - turns * 1.5703125
    rest = rest - turns * 4.837512969970703e-4
    rest = rest - turns * 7.549789948768648e-8
    return in_quarter(turns, rest)


def cos_sin_quarters(quarters):
    turns = jnp.floor(quarters + 0.5)
    return in_quarter(turns, (quarters - turns) * (0.5 * math.pi))


def in_quarter(turns, rest):
    square = rest * rest
    sine = rest + rest * square * (
        -1.6666654611e-1 + square * (8.3321608736e-3 + square * -1.9515295891e-4)
    )
    cosine = (1.0 - 0.5 * square) + square * square * (
        4.166664568298827e-2 + square * (-1.388731625493765e-3 + square * 2.443315711809948e-5)
    )
    quarter = turns.astype(jnp.int32)
    swap = (quarter & 1) != 0
    cos_part = jnp.where(swap, sine, cosine)
    sin_part = jnp.where(swap, cosine, sine)
    cos_part = jnp.where(((quarter + 1) & 2) != 0, -cos_part, cos_part)
    sin_part = jnp.where((quarter & 2) != 0, -sin_part, sin_part)
    return cos_part, sin_part


def times(left, right):
    return (
        left[0] * right[0] - left[1] * right[1],
        left[0] * right[1] + left[1] * right[0],
    )


def times_conj(left, right):
    return (
        left[0] * right[0] + left[1] * right[1],
        left[1] * right[0] - left[0] * right[1],
    )


def plus(left, right):
    return (left[0] + right[0], left[1] + right[1])


def minus(left, right):
    return (left[0] - right[0], left[1] - right[1])


def quarter_turn(value, sign):
    if sign > 0:
        return (-value[1], value[0])
    return (value[1], -value[0])


def dft4(items, sign):
    even, odd = plus(items[0], items[2]), minus(items[0], items[2])
    other, rest = plus(items[1], items[3]), minus(items[1], items[3])
    rest = quarter_turn(rest, sign)
    return [plus(even, other), plus(odd, rest), minus(even, other), minus(odd, rest)]


def dft8(items, sign):
    even, odd = dft4(items[0::2], sign), dft4(items[1::2], sign)
    half = math.sqrt(0.5)
    first, third = odd[1], odd[3]
    if sign > 0:
        first = ((first[0] - first[1]) * half, (first[0] + first[1]) * half)
        third = ((-third[0] - third[1]) * half, (third[0] - third[1]) * half)
    else:
        first = ((first[0] + first[1]) * half, (first[1] - first[0]) * half)
        third = ((third[1] - third[0]) * half, (-third[0] - third[1]) * half)
    odd = [odd[0], first, quarter_turn(odd[2], sign), third]
    return [plus(e, o) for e, o in zip(even, odd)] + [minus(e, o) for e, o in zip(even, odd)]


def matmul_pair(left, right, high, low):
    both = jnp.concatenate([left, right], axis=1)
    upper = both.astype(jnp.bfloat16)
    lower = (both - upper.astype(jnp.float32)).astype(jnp.bfloat16)
    product = functools.partial(jnp.dot, preferred_element_type=jnp.float32)
    result = product(upper, high) + (product(lower, high) + product(upper, low))
    return result[:, :LANES], result[:, LANES:]


def line_filter(field, filters, twist, high, low, sign):
    def stack(items, part):
        return jnp.concatenate([item[part] for item in items], axis=0)

    def pieces(real, imag):
        return [(real[k * CHUNK : (k + 1) * CHUNK], imag[k * CHUNK : (k + 1) * CHUNK]) for k in range(GROUPS)]

    multiply = times if sign > 0 else times_conj
    products = []
    for wave in field:
        for first in range(0, WIDE, CHUNK):
            parts = dft8([(real[first : first + CHUNK], imag[first : first + CHUNK]) for real, imag in wave], -1)
            parts = [parts[0]] + [times(parts[k], twist[k]) for k in range(1, GROUPS)]
            products.append(matmul_pair(stack(parts, 0), stack(parts, 1), high, low))
    returned = []
    for index, product in enumerate(products):
        picks = filters[index // (WIDE // CHUNK)]
        spectrum = [multiply(value, pick) for value, pick in zip(pieces(*product), picks)]
        imag, real = matmul_pair(stack(spectrum, 1), stack(spectrum, 0), high, low)
        returned.append((real, imag))
    chunks = []
    for product in returned:
        parts = pieces(*product)
        parts = [parts[0]] + [times_conj(parts[k], twist[k]) for k in range(1, GROUPS)]
        chunks.append(dft8(parts, 1))
    result = []
    for wave in range(len(field)):
        mine = chunks[wave * (WIDE // CHUNK) : (wave + 1) * (WIDE // CHUNK)]
        result.append(
            [
                tuple(jnp.concatenate([chunk[group][part] for chunk in mine], axis=0) for part in range(2))
                for group in range(GROUPS)
            ]
        )
    return result


def load_field(blocks_ref, start):
    turned = [
        jnp.concatenate([blocks_ref[GROUPS * i + j, start : start + WIDE] for i in range(FOLD)], axis=0).T
        for j in range(GROUPS)
    ]
    field = [[[None, None] for _ in range(GROUPS)] for _ in range(SHARE)]
    for part in range(2):
        for wave in range(SHARE):
            first = (part * SHARE + wave) * WIDE
            for half in range(GROUPS // FOLD):
                rows = [turned[half * FOLD + i][first : first + WIDE] for i in range(FOLD)]
                points = jnp.concatenate(rows, axis=0).T
                for i in range(FOLD):
                    group = i * (GROUPS // FOLD) + half
                    field[wave][group][part] = points[i * WIDE : (i + 1) * WIDE]
    return field


def store_field(blocks_ref, start, field):
    for group in range(GROUPS):
        rows = [field[w][group][part] for part in range(2) for w in range(SHARE)]
        turned = jnp.concatenate(rows, axis=0).T
        for i in range(FOLD):
            blocks_ref[FOLD * group + i, start : start + WIDE] = turned[i * WIDE : (i + 1) * WIDE]


def store_planes(blocks_ref, start, planes):
    lane = lax.broadcasted_iota(jnp.int32, (16, LANES), 1)
    for group in range(GROUPS):
        rows = [planes[0][group], planes[1][group]]
        turned = jnp.concatenate(rows + rows, axis=0).T
        for i in range(FOLD):
            upper, lower = turned[i * WIDE : i * WIDE + 16], turned[i * WIDE + 16 : (i + 1) * WIDE]
            blocks_ref[FOLD * group + i, start : start + 16] = jnp.where(lane < 64, upper, lower)


def load_planes(blocks_ref, start):
    turned = [
        jnp.concatenate([blocks_ref[FOLD * i + j, start : start + 16] for i in range(GROUPS)], axis=0).T
        for j in range(FOLD)
    ]
    planes = []
    for plane in range(2):
        halves = []
        for half in range(2):
            first = (half * 2 + plane) * WIDE
            halves.append(jnp.concatenate([t[first : first + WIDE] for t in turned], axis=0).T)
        planes.append(
            [
                jnp.concatenate([half[16 * group : 16 * (group + 1)] for half in halves], axis=0)
                for group in range(GROUPS)
            ]
        )
    return planes


def ratio_of(place_ref, wave):
    number = place_ref[2 + place_ref[0] * SHARE + wave]
    return ratio_base + ratio_step * number.astype(jnp.float32)


def write_constants(constants_ref, place_ref):
    row = lax.broadcasted_iota(jnp.int32, (GROUPS, LANES), 0)
    lane = lax.broadcasted_iota(jnp.int32, (GROUPS, LANES), 1)
    natural = row + GROUPS * lane
    signed = jnp.where(natural < GRID // 2, natural, natural - GRID)
    scaled = signed.astype(jnp.float32) * (2.0 / GRID)
    squares = scaled * scaled
    for wave in range(SHARE):
        ratio = ratio_of(place_ref, wave)
        real, imag = cos_sin((-prop_scale * ratio) * squares)
        constants_ref[2 * wave], constants_ref[2 * wave + 1] = real * (1.0 / GRID), imag * (1.0 / GRID)
        constants_ref[2 * SHARE + 2 + wave] = 1.0 / jnp.full((GROUPS, LANES), ratio, jnp.float32)
    real, imag = cos_sin((-2.0 * math.pi / GRID) * (row * lane).astype(jnp.float32))
    constants_ref[2 * SHARE], constants_ref[2 * SHARE + 1] = real, imag


class Constants:
    def __init__(self, constants_ref, high_ref, low_ref):
        def rows(real, imag):
            real, imag = constants_ref[real], constants_ref[imag]
            return [(real[k : k + 1], imag[k : k + 1]) for k in range(GROUPS)]

        self.filters = [rows(2 * wave, 2 * wave + 1) for wave in range(SHARE)]
        self.twist = rows(2 * SHARE, 2 * SHARE + 1)
        self.inverse = [constants_ref[2 * SHARE + 2 + wave][:1] for wave in range(SHARE)]
        self.high, self.low = high_ref[...], low_ref[...]

    def along(self, field, sign):
        return line_filter(field, self.filters, self.twist, self.high, self.low, sign)


def copies(pairs, sems):
    return [pltpu.make_async_copy(source, target, sems.at[i]) for i, (source, target) in enumerate(pairs)]


def start(moves):
    for move in moves:
        move.start()


def wait(moves):
    for move in moves:
        move.wait()


def launch_kernel(
    waves,
    place_ref,
    illum_hbm,
    high_hbm,
    low_hbm,
    measured_hbm,
    out_ref,
    target_ref,
    constants_ref,
    illum_ref,
    high_ref,
    low_ref,
    measured_ref,
    sems,
):
    own = measured_hbm.at[pl.ds(place_ref[0] * SHARE, SHARE)]
    moves = copies(
        [(illum_hbm, illum_ref), (high_hbm, high_ref), (low_hbm, low_ref), (own, measured_ref)], sems
    )
    start(moves)
    write_constants(constants_ref, place_ref)
    tilted = []
    for wave in range(SHARE):
        pick = place_ref[2 + waves + place_ref[0] * SHARE + wave]
        tilt_x = ((pick & (angle_side - 1)) - angle_side // 2) * tilt_step
        tilt_y = ((pick >> 3) - angle_side // 2) * tilt_step
        row = lax.broadcasted_iota(jnp.int32, (WIDE, LANES), 0) + place_ref[1] * WIDE

        def wheel(product):
            turned = ((product + GRID // 2) & (GRID - 1)) - GRID // 2
            return cos_sin((2.0 * math.pi / GRID) * turned.astype(jnp.float32))

        down = wheel(tilt_y * row)
        groups = []
        for group in range(GROUPS):
            column = lax.broadcasted_iota(jnp.int32, (8, LANES), 1) + group * LANES
            across = wheel(tilt_x * column)
            groups.append(times(down, (across[0][:1], across[1][:1])))
        tilted.append(groups)
    wait(moves[:3])
    field = []
    for wave in range(SHARE):
        groups = []
        for group in range(GROUPS):
            bright = illum_ref[:, group * LANES : (group + 1) * LANES]
            groups.append((bright * tilted[wave][group][0], bright * tilted[wave][group][1]))
        field.append(groups)
    store_field(out_ref, 0, Constants(constants_ref, high_ref, low_ref).along(field, 1))
    wait(moves[3:])
    for wave in range(SHARE):
        for part in range(2):
            target_ref[wave, part] = measured_ref[wave, :, part]


def save(kept_ref, field):
    for wave in range(SHARE):
        for group in range(GROUPS):
            for part in range(2):
                kept_ref[wave, group, part] = field[wave][group][part]


def kept(kept_ref):
    return [
        [(kept_ref[wave, group, 0], kept_ref[wave, group, 1]) for group in range(GROUPS)]
        for wave in range(SHARE)
    ]


def screens(base, constants):
    result = []
    for wave in range(SHARE):
        scale = constants.inverse[wave] * (2.0 / math.pi)
        result.append([cos_sin_quarters(plane * scale) for plane in base])
    return result


def gradient(target, field, constants):
    total = [None] * GROUPS
    for wave in range(SHARE):
        scale = constants.inverse[wave]
        for group in range(GROUPS):
            left, right = target[wave][group], field[wave][group]
            term = (left[0] * right[1] - left[1] * right[0]) * scale
            total[group] = term if wave == 0 else total[group] + term
    return total


def lanes_of(group):
    return slice(group * LANES, (group + 1) * LANES)


def planes_of(ref):
    return [ref[:, lanes_of(group)] for group in range(GROUPS)]


def target_of(target_ref):
    return [
        [(target_ref[wave, 0, :, lanes_of(group)], target_ref[wave, 1, :, lanes_of(group)]) for group in range(GROUPS)]
        for wave in range(SHARE)
    ]


def each(function, left, right):
    return [[function(a, b) for a, b in zip(p, q)] for p, q in zip(left, right)]


def begin_kernel(
    constants_ref, launched_ref, slices_ref, mask_ref, target_ref, high_ref, low_ref, out_ref, base_ref, screen_ref
):
    constants = Constants(constants_ref, high_ref, low_ref)
    mask = [core_step * mask_ref[:, lanes_of(group)].astype(jnp.float32) for group in range(GROUPS)]

    def base_of(layer):
        return [mask[group] + slices_ref[layer, :, lanes_of(group)] for group in range(GROUPS)]

    for peer in range(PEERS):
        out_ref[peer, :WIDE] = launched_ref[peer]
    store_planes(out_ref, 2 * WIDE, (base_of(0), base_of(2)))
    for group, plane in enumerate(base_of(1)):
        base_ref[:, lanes_of(group)] = plane
    screen = screens(base_of(3), constants)
    save(screen_ref, screen)
    target = each(times_conj, target_of(target_ref), screen)
    store_field(out_ref, WIDE, constants.along(target, -1))


def first_kernel(constants_ref, in_ref, high_ref, low_ref, out_ref, field_ref, target_ref, screen_ref):
    constants = Constants(constants_ref, high_ref, low_ref)
    base_0, base_2 = load_planes(in_ref, 2 * WIDE)
    field = constants.along(load_field(in_ref, 0), 1)
    field = each(times, field, screens(base_0, constants))
    save(field_ref, field)
    store_field(out_ref, 0, constants.along(field, 1))
    target = constants.along(load_field(in_ref, WIDE), -1)
    save(target_ref, target)
    screen = screens(base_2, constants)
    save(screen_ref, screen)
    target = each(times_conj, target, screen)
    store_field(out_ref, WIDE, constants.along(target, -1))


def second_kernel(constants_ref, in_ref, high_ref, low_ref, base_ref, out_ref, grad_ref):
    constants = Constants(constants_ref, high_ref, low_ref)
    screen = screens(planes_of(base_ref), constants)
    field = constants.along(load_field(in_ref, 0), 1)
    field = each(times, field, screen)
    target = constants.along(load_field(in_ref, WIDE), -1)
    for group, plane in enumerate(gradient(target, field, constants)):
        grad_ref[:, lanes_of(group)] = plane
    store_field(out_ref, 0, constants.along(field, 1))
    target = each(times_conj, target, screen)
    store_field(out_ref, WIDE, constants.along(target, -1))


def third_kernel(constants_ref, in_ref, high_ref, low_ref, field_ref, target_ref, screen_ref, out_ref):
    constants = Constants(constants_ref, high_ref, low_ref)
    field = constants.along(load_field(in_ref, 0), 1)
    field = each(times, field, kept(screen_ref))
    grad_2 = gradient(kept(target_ref), field, constants)
    store_field(out_ref, 0, constants.along(field, 1))
    target = constants.along(load_field(in_ref, WIDE), -1)
    store_planes(out_ref, WIDE, (gradient(target, kept(field_ref), constants), grad_2))


def last_kernel(constants_ref, in_ref, high_ref, low_ref, screen_ref, target_ref, first_ref, out_ref):
    constants = Constants(constants_ref, high_ref, low_ref)
    field = constants.along(load_field(in_ref, 0), 1)
    field = each(times, field, kept(screen_ref))
    grad_0, grad_2 = load_planes(in_ref, WIDE)
    planes = [grad_0, planes_of(first_ref), grad_2, gradient(target_of(target_ref), field, constants)]
    for layer, plane in enumerate(planes):
        for group in range(GROUPS):
            out_ref[layer, :, lanes_of(group)] = plane[group]


def sum_kernel(in_ref, out_ref):
    total = in_ref[0]
    for section in range(1, in_ref.shape[0]):
        total = total + in_ref[section]
    out_ref[0] = total


def call(kernel, scalars, near, far, outs, scratch=(), moves=1):
    specs = [pl.BlockSpec(memory_space=pltpu.SMEM)] * len(scalars)
    specs += [pl.BlockSpec(memory_space=pltpu.VMEM)] * len(near)
    specs += [pl.BlockSpec(memory_space=pltpu.HBM)] * len(far)
    scratch = [pltpu.VMEM(shape, dtype) for shape, dtype in scratch]
    if scratch:
        scratch.append(pltpu.SemaphoreType.DMA((moves,)))
    return pl.pallas_call(
        kernel,
        out_shape=[place(shape, jnp.float32) for shape, place in outs],
        in_specs=specs,
        out_specs=[pl.BlockSpec(memory_space=pltpu.VMEM)] * len(outs),
        scratch_shapes=scratch,
        compiler_params=pltpu.CompilerParams(vmem_limit_bytes=VMEM_LIMIT),
    )(*scalars, *near, *far)


def near(shape):
    return (shape, pltpu.VMEM)


def free(shape):
    return (shape, jax.ShapeDtypeStruct)


def in_hbm(*arrays):
    return tuple(pltpu.with_memory_space_constraint(array, pltpu.HBM) for array in arrays)


def body(index_slices, core_mask, illum_amp, measured, wave_ids, angle_ids):
    row_pos, sec_pos = lax.axis_index("row"), lax.axis_index("sec")
    sec_count, waves = lax.axis_size("sec"), wave_ids.shape[0]
    tables = tuple(jnp.asarray(table) for table in dft_tables())
    place = jnp.concatenate([sec_pos[None], row_pos[None], wave_ids, angle_ids]).astype(jnp.int32)
    swap = functools.partial(lax.all_to_all, split_axis=0, concat_axis=0, tiled=True)
    plane, saved = (WIDE, GRID), (SHARE, GROUPS, 2, WIDE, LANES)
    table = ((2 * LANES, 2 * LANES), jnp.bfloat16)

    def blocks(rows):
        return free((PEERS, rows, LANES))

    slices = swap(jnp.broadcast_to(index_slices, (sec_count, *plane)), "sec")
    launched, target, constants = call(
        functools.partial(launch_kernel, waves),
        (place,),
        (),
        in_hbm(illum_amp, *tables, measured),
        (near((PEERS, WIDE, LANES)), near((SHARE, 2, *plane)), near((3 * SHARE + 2, GROUPS, LANES))),
        scratch=((plane, jnp.float32), table, table, ((SHARE, *measured.shape[1:]), jnp.float32)),
        moves=4,
    )
    sent, base, screen_3 = call(
        begin_kernel,
        (),
        (constants, launched, slices, core_mask, target, *tables),
        (),
        (blocks(2 * WIDE + 16), near(plane), near(saved)),
    )
    sent, field_0, target_2, screen_2 = call(
        first_kernel, (), (constants, swap(sent, "row"), *tables), (), (blocks(2 * WIDE),) + (near(saved),) * 3
    )
    sent, grad_1 = call(
        second_kernel, (), (constants, swap(sent, "row"), *tables, base), (), (blocks(2 * WIDE), near(plane))
    )
    (sent,) = call(
        third_kernel,
        (),
        (constants, swap(sent, "row"), *tables, field_0, target_2, screen_2),
        (),
        (blocks(WIDE + 16),),
    )
    (grads,) = call(
        last_kernel,
        (),
        (constants, swap(sent, "row"), *tables, screen_3, target, grad_1),
        (),
        (free((sec_count, *plane)),),
    )
    (result,) = call(sum_kernel, (), (swap(grads, "sec"),), (), (free((1, *plane)),))
    return result


def solution(mesh):
    in_specs = (
        P("sec", "row", None),
        P("row", None),
        P("row", None),
        P(None, "row", None, None),
        P(),
        P(),
    )
    out_specs = P("sec", "row", None)
    return jax.shard_map(body, mesh=mesh, in_specs=in_specs, out_specs=out_specs, check_vma=False)
```

```python
import functools
import math

import jax
import jax.numpy as jnp
import numpy as np
from jax import lax
from jax.experimental import pallas as pl
from jax.experimental.pallas import tpu as pltpu
from jax.sharding import PartitionSpec as P

ratio_base = 0.75
ratio_step = 1.0 / 128.0
prop_scale = 150.0
core_step = 0.8
tilt_step = 8
angle_side = 8

LANES = 128
GROUPS = 8
GRID = GROUPS * LANES
WIDE = 32
PEERS = GRID // WIDE
SHARE = 2
FOLD = LANES // WIDE
CHUNK = 16
VMEM_LIMIT = 48 * 1024 * 1024


def dft_tables():
    counter = np.arange(LANES)
    angle = -2.0 * np.pi / LANES * (counter[:, None] * counter[None, :] % LANES)
    real, imag = np.cos(angle), np.sin(angle)
    full = np.block([[real, imag], [-imag, real]]).astype(np.float32)
    high = full.astype(jnp.bfloat16)
    low = (full - high.astype(np.float32)).astype(jnp.bfloat16)
    return high, low


def cos_sin(angle):
    turns = jnp.floor(angle * (2.0 / math.pi) + 0.5)
    rest = angle - turns * 1.5703125
    rest = rest - turns * 4.837512969970703e-4
    rest = rest - turns * 7.549789948768648e-8
    return in_quarter(turns, rest)


def cos_sin_quarters(quarters):
    turns = jnp.floor(quarters + 0.5)
    return in_quarter(turns, (quarters - turns) * (0.5 * math.pi))


def in_quarter(turns, rest):
    square = rest * rest
    sine = rest + rest * square * (
        -1.6666654611e-1 + square * (8.3321608736e-3 + square * -1.9515295891e-4)
    )
    cosine = (1.0 - 0.5 * square) + square * square * (
        4.166664568298827e-2 + square * (-1.388731625493765e-3 + square * 2.443315711809948e-5)
    )
    quarter = turns.astype(jnp.int32)
    swap = (quarter & 1) != 0
    cos_part = jnp.where(swap, sine, cosine)
    sin_part = jnp.where(swap, cosine, sine)
    cos_part = jnp.where(((quarter + 1) & 2) != 0, -cos_part, cos_part)
    sin_part = jnp.where((quarter & 2) != 0, -sin_part, sin_part)
    return cos_part, sin_part


def times(left, right):
    return (
        left[0] * right[0] - left[1] * right[1],
        left[0] * right[1] + left[1] * right[0],
    )


def times_conj(left, right):
    return (
        left[0] * right[0] + left[1] * right[1],
        left[1] * right[0] - left[0] * right[1],
    )


def plus(left, right):
    return (left[0] + right[0], left[1] + right[1])


def minus(left, right):
    return (left[0] - right[0], left[1] - right[1])


def quarter_turn(value, sign):
    if sign > 0:
        return (-value[1], value[0])
    return (value[1], -value[0])


def dft4(items, sign):
    even, odd = plus(items[0], items[2]), minus(items[0], items[2])
    other, rest = plus(items[1], items[3]), minus(items[1], items[3])
    rest = quarter_turn(rest, sign)
    return [plus(even, other), plus(odd, rest), minus(even, other), minus(odd, rest)]


def dft8(items, sign):
    even, odd = dft4(items[0::2], sign), dft4(items[1::2], sign)
    half = math.sqrt(0.5)
    first, third = odd[1], odd[3]
    if sign > 0:
        first = ((first[0] - first[1]) * half, (first[0] + first[1]) * half)
        third = ((-third[0] - third[1]) * half, (third[0] - third[1]) * half)
    else:
        first = ((first[0] + first[1]) * half, (first[1] - first[0]) * half)
        third = ((third[1] - third[0]) * half, (-third[0] - third[1]) * half)
    odd = [odd[0], first, quarter_turn(odd[2], sign), third]
    return [plus(e, o) for e, o in zip(even, odd)] + [minus(e, o) for e, o in zip(even, odd)]


def matmul_pair(left, right, high, low):
    both = jnp.concatenate([left, right], axis=1)
    upper = both.astype(jnp.bfloat16)
    lower = (both - upper.astype(jnp.float32)).astype(jnp.bfloat16)
    product = functools.partial(jnp.dot, preferred_element_type=jnp.float32)
    result = product(upper, high) + (product(lower, high) + product(upper, low))
    return result[:, :LANES], result[:, LANES:]


def line_filter(field, filters, twist, high, low, sign):
    def stack(items, part):
        return jnp.concatenate([item[part] for item in items], axis=0)

    def pieces(real, imag):
        return [(real[k * CHUNK : (k + 1) * CHUNK], imag[k * CHUNK : (k + 1) * CHUNK]) for k in range(GROUPS)]

    multiply = times if sign > 0 else times_conj
    products = []
    for wave in field:
        for first in range(0, WIDE, CHUNK):
            parts = dft8([(real[first : first + CHUNK], imag[first : first + CHUNK]) for real, imag in wave], -1)
            parts = [parts[0]] + [times(parts[k], twist[k]) for k in range(1, GROUPS)]
            products.append(matmul_pair(stack(parts, 0), stack(parts, 1), high, low))
    returned = []
    for index, product in enumerate(products):
        picks = filters[index // (WIDE // CHUNK)]
        spectrum = [multiply(value, pick) for value, pick in zip(pieces(*product), picks)]
        imag, real = matmul_pair(stack(spectrum, 1), stack(spectrum, 0), high, low)
        returned.append((real, imag))
    chunks = []
    for product in returned:
        parts = pieces(*product)
        parts = [parts[0]] + [times_conj(parts[k], twist[k]) for k in range(1, GROUPS)]
        chunks.append(dft8(parts, 1))
    result = []
    for wave in range(len(field)):
        mine = chunks[wave * (WIDE // CHUNK) : (wave + 1) * (WIDE // CHUNK)]
        result.append(
            [
                tuple(jnp.concatenate([chunk[group][part] for chunk in mine], axis=0) for part in range(2))
                for group in range(GROUPS)
            ]
        )
    return result


def load_field(blocks_ref, start):
    turned = [
        jnp.concatenate([blocks_ref[GROUPS * i + j, start : start + WIDE] for i in range(FOLD)], axis=0).T
        for j in range(GROUPS)
    ]
    field = [[[None, None] for _ in range(GROUPS)] for _ in range(SHARE)]
    for part in range(2):
        for wave in range(SHARE):
            first = (part * SHARE + wave) * WIDE
            for half in range(GROUPS // FOLD):
                rows = [turned[half * FOLD + i][first : first + WIDE] for i in range(FOLD)]
                points = jnp.concatenate(rows, axis=0).T
                for i in range(FOLD):
                    group = i * (GROUPS // FOLD) + half
                    field[wave][group][part] = points[i * WIDE : (i + 1) * WIDE]
    return field


def store_field(blocks_ref, start, field):
    for group in range(GROUPS):
        rows = [field[w][group][part] for part in range(2) for w in range(SHARE)]
        turned = jnp.concatenate(rows, axis=0).T
        for i in range(FOLD):
            blocks_ref[FOLD * group + i, start : start + WIDE] = turned[i * WIDE : (i + 1) * WIDE]


def store_planes(blocks_ref, start, planes):
    lane = lax.broadcasted_iota(jnp.int32, (16, LANES), 1)
    for group in range(GROUPS):
        rows = [planes[0][group], planes[1][group]]
        turned = jnp.concatenate(rows + rows, axis=0).T
        for i in range(FOLD):
            upper, lower = turned[i * WIDE : i * WIDE + 16], turned[i * WIDE + 16 : (i + 1) * WIDE]
            blocks_ref[FOLD * group + i, start : start + 16] = jnp.where(lane < 64, upper, lower)


def load_planes(blocks_ref, start):
    turned = [
        jnp.concatenate([blocks_ref[FOLD * i + j, start : start + 16] for i in range(GROUPS)], axis=0).T
        for j in range(FOLD)
    ]
    planes = []
    for plane in range(2):
        halves = []
        for half in range(2):
            first = (half * 2 + plane) * WIDE
            halves.append(jnp.concatenate([t[first : first + WIDE] for t in turned], axis=0).T)
        planes.append(
            [
                jnp.concatenate([half[16 * group : 16 * (group + 1)] for half in halves], axis=0)
                for group in range(GROUPS)
            ]
        )
    return planes


def ratio_of(place_ref, wave):
    number = place_ref[2 + place_ref[0] * SHARE + wave]
    return ratio_base + ratio_step * number.astype(jnp.float32)


def write_constants(constants_ref, place_ref):
    row = lax.broadcasted_iota(jnp.int32, (GROUPS, LANES), 0)
    lane = lax.broadcasted_iota(jnp.int32, (GROUPS, LANES), 1)
    natural = row + GROUPS * lane
    signed = jnp.where(natural < GRID // 2, natural, natural - GRID)
    scaled = signed.astype(jnp.float32) * (2.0 / GRID)
    squares = scaled * scaled
    for wave in range(SHARE):
        ratio = ratio_of(place_ref, wave)
        real, imag = cos_sin((-prop_scale * ratio) * squares)
        constants_ref[2 * wave], constants_ref[2 * wave + 1] = real * (1.0 / GRID), imag * (1.0 / GRID)
        constants_ref[2 * SHARE + 2 + wave] = 1.0 / jnp.full((GROUPS, LANES), ratio, jnp.float32)
    constants_ref[3 * SHARE + 2] = jnp.full((GROUPS, LANES), place_ref[0].astype(jnp.float32), jnp.float32)
    real, imag = cos_sin((-2.0 * math.pi / GRID) * (row * lane).astype(jnp.float32))
    constants_ref[2 * SHARE], constants_ref[2 * SHARE + 1] = real, imag


class Constants:
    def __init__(self, constants_ref, high_ref, low_ref):
        def rows(real, imag):
            real, imag = constants_ref[real], constants_ref[imag]
            return [(real[k : k + 1], imag[k : k + 1]) for k in range(GROUPS)]

        self.filters = [rows(2 * wave, 2 * wave + 1) for wave in range(SHARE)]
        self.twist = rows(2 * SHARE, 2 * SHARE + 1)
        self.inverse = [constants_ref[2 * SHARE + 2 + wave][:1] for wave in range(SHARE)]
        self.high, self.low = high_ref[...], low_ref[...]

    def along(self, field, sign):
        return line_filter(field, self.filters, self.twist, self.high, self.low, sign)


def copies(pairs, sems):
    return [pltpu.make_async_copy(source, target, sems.at[i]) for i, (source, target) in enumerate(pairs)]


def start(moves):
    for move in moves:
        move.start()


def wait(moves):
    for move in moves:
        move.wait()


def launch_kernel(
    waves,
    place_ref,
    illum_hbm,
    high_hbm,
    low_hbm,
    measured_hbm,
    out_ref,
    target_ref,
    constants_ref,
    illum_ref,
    high_ref,
    low_ref,
    measured_ref,
    sems,
):
    own = measured_hbm.at[pl.ds(place_ref[0] * SHARE, SHARE)]
    moves = copies(
        [(illum_hbm, illum_ref), (high_hbm, high_ref), (low_hbm, low_ref), (own, measured_ref)], sems
    )
    start(moves)
    write_constants(constants_ref, place_ref)
    tilted = []
    for wave in range(SHARE):
        pick = place_ref[2 + waves + place_ref[0] * SHARE + wave]
        tilt_x = ((pick & (angle_side - 1)) - angle_side // 2) * tilt_step
        tilt_y = ((pick >> 3) - angle_side // 2) * tilt_step
        row = lax.broadcasted_iota(jnp.int32, (WIDE, LANES), 0) + place_ref[1] * WIDE

        def wheel(product):
            turned = ((product + GRID // 2) & (GRID - 1)) - GRID // 2
            return cos_sin((2.0 * math.pi / GRID) * turned.astype(jnp.float32))

        down = wheel(tilt_y * row)
        groups = []
        for group in range(GROUPS):
            column = lax.broadcasted_iota(jnp.int32, (8, LANES), 1) + group * LANES
            across = wheel(tilt_x * column)
            groups.append(times(down, (across[0][:1], across[1][:1])))
        tilted.append(groups)
    wait(moves[:3])
    field = []
    for wave in range(SHARE):
        groups = []
        for group in range(GROUPS):
            bright = illum_ref[:, group * LANES : (group + 1) * LANES]
            groups.append((bright * tilted[wave][group][0], bright * tilted[wave][group][1]))
        field.append(groups)
    store_field(out_ref, 0, Constants(constants_ref, high_ref, low_ref).along(field, 1))
    wait(moves[3:])
    for wave in range(SHARE):
        for part in range(2):
            target_ref[wave, part] = measured_ref[wave, :, part]


def save(kept_ref, field):
    for wave in range(SHARE):
        for group in range(GROUPS):
            for part in range(2):
                kept_ref[wave, group, part] = field[wave][group][part]


def kept(kept_ref):
    return [
        [(kept_ref[wave, group, 0], kept_ref[wave, group, 1]) for group in range(GROUPS)]
        for wave in range(SHARE)
    ]


def screens(base, constants):
    result = []
    for wave in range(SHARE):
        scale = constants.inverse[wave] * (2.0 / math.pi)
        result.append([cos_sin_quarters(plane * scale) for plane in base])
    return result


def gradient(target, field, constants):
    total = [None] * GROUPS
    for wave in range(SHARE):
        scale = constants.inverse[wave]
        for group in range(GROUPS):
            left, right = target[wave][group], field[wave][group]
            term = (left[0] * right[1] - left[1] * right[0]) * scale
            total[group] = term if wave == 0 else total[group] + term
    return total


def lanes_of(group):
    return slice(group * LANES, (group + 1) * LANES)


def planes_of(ref):
    return [ref[:, lanes_of(group)] for group in range(GROUPS)]


def target_of(target_ref):
    return [
        [(target_ref[wave, 0, :, lanes_of(group)], target_ref[wave, 1, :, lanes_of(group)]) for group in range(GROUPS)]
        for wave in range(SHARE)
    ]


def each(function, left, right):
    return [[function(a, b) for a, b in zip(p, q)] for p, q in zip(left, right)]


def begin_kernel(
    constants_ref,
    launched_ref,
    slice_0,
    slice_1,
    slice_2,
    slice_3,
    mask_ref,
    target_ref,
    high_ref,
    low_ref,
    out_ref,
    base_ref,
    screen_ref,
):
    constants = Constants(constants_ref, high_ref, low_ref)
    mask = [core_step * mask_ref[:, lanes_of(group)].astype(jnp.float32) for group in range(GROUPS)]

    def base_of(layer):
        back = constants_ref[3 * SHARE + 2][:1] - float(layer)
        back = jnp.where(back < 0.0, back + 4.0, back)
        result = []
        for group in range(GROUPS):
            value = slice_0[0, :, lanes_of(group)]
            for place, ref in enumerate((slice_1, slice_2, slice_3)):
                value = jnp.where(back == place + 1.0, ref[0, :, lanes_of(group)], value)
            result.append(mask[group] + value)
        return result

    for peer in range(PEERS):
        out_ref[peer, :WIDE] = launched_ref[peer]
    store_planes(out_ref, 2 * WIDE, (base_of(0), base_of(2)))
    for group, plane in enumerate(base_of(1)):
        base_ref[:, lanes_of(group)] = plane
    screen = screens(base_of(3), constants)
    save(screen_ref, screen)
    target = each(times_conj, target_of(target_ref), screen)
    store_field(out_ref, WIDE, constants.along(target, -1))


def first_kernel(constants_ref, in_ref, high_ref, low_ref, out_ref, field_ref, target_ref, screen_ref):
    constants = Constants(constants_ref, high_ref, low_ref)
    base_0, base_2 = load_planes(in_ref, 2 * WIDE)
    field = constants.along(load_field(in_ref, 0), 1)
    field = each(times, field, screens(base_0, constants))
    save(field_ref, field)
    store_field(out_ref, 0, constants.along(field, 1))
    target = constants.along(load_field(in_ref, WIDE), -1)
    save(target_ref, target)
    screen = screens(base_2, constants)
    save(screen_ref, screen)
    target = each(times_conj, target, screen)
    store_field(out_ref, WIDE, constants.along(target, -1))


def second_kernel(constants_ref, in_ref, high_ref, low_ref, base_ref, out_ref, grad_ref):
    constants = Constants(constants_ref, high_ref, low_ref)
    screen = screens(planes_of(base_ref), constants)
    field = constants.along(load_field(in_ref, 0), 1)
    field = each(times, field, screen)
    target = constants.along(load_field(in_ref, WIDE), -1)
    for group, plane in enumerate(gradient(target, field, constants)):
        grad_ref[:, lanes_of(group)] = plane
    store_field(out_ref, 0, constants.along(field, 1))
    target = each(times_conj, target, screen)
    store_field(out_ref, WIDE, constants.along(target, -1))


def third_kernel(constants_ref, in_ref, high_ref, low_ref, field_ref, target_ref, screen_ref, out_ref):
    constants = Constants(constants_ref, high_ref, low_ref)
    field = constants.along(load_field(in_ref, 0), 1)
    field = each(times, field, kept(screen_ref))
    grad_2 = gradient(kept(target_ref), field, constants)
    store_field(out_ref, 0, constants.along(field, 1))
    target = constants.along(load_field(in_ref, WIDE), -1)
    store_planes(out_ref, WIDE, (gradient(target, kept(field_ref), constants), grad_2))


def last_kernel(constants_ref, in_ref, high_ref, low_ref, screen_ref, target_ref, first_ref, out_ref):
    constants = Constants(constants_ref, high_ref, low_ref)
    field = constants.along(load_field(in_ref, 0), 1)
    field = each(times, field, kept(screen_ref))
    grad_0, grad_2 = load_planes(in_ref, WIDE)
    planes = [grad_0, planes_of(first_ref), grad_2, gradient(target_of(target_ref), field, constants)]
    for layer, plane in enumerate(planes):
        for group in range(GROUPS):
            out_ref[layer, :, lanes_of(group)] = plane[group]


def sum_kernel(in_ref, out_ref):
    total = in_ref[0]
    for section in range(1, in_ref.shape[0]):
        total = total + in_ref[section]
    out_ref[0] = total


def call(kernel, scalars, near, far, outs, scratch=(), moves=1):
    specs = [pl.BlockSpec(memory_space=pltpu.SMEM)] * len(scalars)
    specs += [pl.BlockSpec(memory_space=pltpu.VMEM)] * len(near)
    specs += [pl.BlockSpec(memory_space=pltpu.HBM)] * len(far)
    scratch = [pltpu.VMEM(shape, dtype) for shape, dtype in scratch]
    if scratch:
        scratch.append(pltpu.SemaphoreType.DMA((moves,)))
    return pl.pallas_call(
        kernel,
        out_shape=[place(shape, jnp.float32) for shape, place in outs],
        in_specs=specs,
        out_specs=[pl.BlockSpec(memory_space=pltpu.VMEM)] * len(outs),
        scratch_shapes=scratch,
        compiler_params=pltpu.CompilerParams(vmem_limit_bytes=VMEM_LIMIT),
    )(*scalars, *near, *far)


def near(shape):
    return (shape, pltpu.VMEM)


def free(shape):
    return (shape, jax.ShapeDtypeStruct)


def in_hbm(*arrays):
    return tuple(pltpu.with_memory_space_constraint(array, pltpu.HBM) for array in arrays)


def body(index_slices, core_mask, illum_amp, measured, wave_ids, angle_ids):
    row_pos, sec_pos = lax.axis_index("row"), lax.axis_index("sec")
    sec_count, waves = lax.axis_size("sec"), wave_ids.shape[0]
    tables = tuple(jnp.asarray(table) for table in dft_tables())
    place = jnp.concatenate([sec_pos[None], row_pos[None], wave_ids, angle_ids]).astype(jnp.int32)
    swap = functools.partial(lax.all_to_all, split_axis=0, concat_axis=0, tiled=True)
    plane, saved = (WIDE, GRID), (SHARE, GROUPS, 2, WIDE, LANES)
    table = ((2 * LANES, 2 * LANES), jnp.bfloat16)

    def blocks(rows):
        return free((PEERS, rows, LANES))

    slices = [index_slices]
    for back in range(1, sec_count):
        pairs = [(i, (i + back) % sec_count) for i in range(sec_count)]
        slices.append(lax.ppermute(index_slices, "sec", pairs))
    launched, target, constants = call(
        functools.partial(launch_kernel, waves),
        (place,),
        (),
        in_hbm(illum_amp, *tables, measured),
        (near((PEERS, WIDE, LANES)), near((SHARE, 2, *plane)), near((3 * SHARE + 3, GROUPS, LANES))),
        scratch=((plane, jnp.float32), table, table, ((SHARE, *measured.shape[1:]), jnp.float32)),
        moves=4,
    )
    sent, base, screen_3 = call(
        begin_kernel,
        (),
        (constants, launched, *slices, core_mask, target, *tables),
        (),
        (blocks(2 * WIDE + 16), near(plane), near(saved)),
    )
    sent, field_0, target_2, screen_2 = call(
        first_kernel, (), (constants, swap(sent, "row"), *tables), (), (blocks(2 * WIDE),) + (near(saved),) * 3
    )
    sent, grad_1 = call(
        second_kernel, (), (constants, swap(sent, "row"), *tables, base), (), (blocks(2 * WIDE), near(plane))
    )
    (sent,) = call(
        third_kernel,
        (),
        (constants, swap(sent, "row"), *tables, field_0, target_2, screen_2),
        (),
        (blocks(WIDE + 16),),
    )
    (grads,) = call(
        last_kernel,
        (),
        (constants, swap(sent, "row"), *tables, screen_3, target, grad_1),
        (),
        (free((sec_count, *plane)),),
    )
    (result,) = call(sum_kernel, (), (swap(grads, "sec"),), (), (free((1, *plane)),))
    return result


def solution(mesh):
    in_specs = (
        P("sec", "row", None),
        P("row", None),
        P("row", None),
        P(None, "row", None, None),
        P(),
        P(),
    )
    out_specs = P("sec", "row", None)
    return jax.shard_map(body, mesh=mesh, in_specs=in_specs, out_specs=out_specs, check_vma=False)
```

```python
import functools
import math

import jax
import jax.numpy as jnp
import numpy as np
from jax import lax
from jax.experimental import pallas as pl
from jax.experimental.pallas import tpu as pltpu
from jax.sharding import PartitionSpec as P

ratio_base = 0.75
ratio_step = 1.0 / 128.0
prop_scale = 150.0
core_step = 0.8
tilt_step = 8
angle_side = 8

LANES = 128
GROUPS = 8
GRID = GROUPS * LANES
WIDE = 32
PEERS = GRID // WIDE
SHARE = 2
FOLD = LANES // WIDE
CHUNK = 16
VMEM_LIMIT = 48 * 1024 * 1024


def dft_tables():
    counter = np.arange(LANES)
    angle = -2.0 * np.pi / LANES * (counter[:, None] * counter[None, :] % LANES)
    real, imag = np.cos(angle), np.sin(angle)
    full = np.block([[real, imag], [-imag, real]]).astype(np.float32)
    high = full.astype(jnp.bfloat16)
    low = (full - high.astype(np.float32)).astype(jnp.bfloat16)
    return high, low


def cos_sin(angle):
    turns = jnp.floor(angle * (2.0 / math.pi) + 0.5)
    rest = angle - turns * 1.5703125
    rest = rest - turns * 4.837512969970703e-4
    rest = rest - turns * 7.549789948768648e-8
    return in_quarter(turns, rest)


def cos_sin_quarters(quarters):
    turns = jnp.floor(quarters + 0.5)
    return in_quarter(turns, (quarters - turns) * (0.5 * math.pi))


def in_quarter(turns, rest):
    square = rest * rest
    sine = rest + rest * square * (
        -1.6666654611e-1 + square * (8.3321608736e-3 + square * -1.9515295891e-4)
    )
    cosine = (1.0 - 0.5 * square) + square * square * (
        4.166664568298827e-2 + square * (-1.388731625493765e-3 + square * 2.443315711809948e-5)
    )
    quarter = turns.astype(jnp.int32)
    swap = (quarter & 1) != 0
    cos_part = jnp.where(swap, sine, cosine)
    sin_part = jnp.where(swap, cosine, sine)
    cos_part = jnp.where(((quarter + 1) & 2) != 0, -cos_part, cos_part)
    sin_part = jnp.where((quarter & 2) != 0, -sin_part, sin_part)
    return cos_part, sin_part


def times(left, right):
    return (
        left[0] * right[0] - left[1] * right[1],
        left[0] * right[1] + left[1] * right[0],
    )


def times_conj(left, right):
    return (
        left[0] * right[0] + left[1] * right[1],
        left[1] * right[0] - left[0] * right[1],
    )


def plus(left, right):
    return (left[0] + right[0], left[1] + right[1])


def minus(left, right):
    return (left[0] - right[0], left[1] - right[1])


def quarter_turn(value, sign):
    if sign > 0:
        return (-value[1], value[0])
    return (value[1], -value[0])


def dft4(items, sign):
    even, odd = plus(items[0], items[2]), minus(items[0], items[2])
    other, rest = plus(items[1], items[3]), minus(items[1], items[3])
    rest = quarter_turn(rest, sign)
    return [plus(even, other), plus(odd, rest), minus(even, other), minus(odd, rest)]


def dft8(items, sign):
    even, odd = dft4(items[0::2], sign), dft4(items[1::2], sign)
    half = math.sqrt(0.5)
    first, third = odd[1], odd[3]
    if sign > 0:
        first = ((first[0] - first[1]) * half, (first[0] + first[1]) * half)
        third = ((-third[0] - third[1]) * half, (third[0] - third[1]) * half)
    else:
        first = ((first[0] + first[1]) * half, (first[1] - first[0]) * half)
        third = ((third[1] - third[0]) * half, (-third[0] - third[1]) * half)
    odd = [odd[0], first, quarter_turn(odd[2], sign), third]
    return [plus(e, o) for e, o in zip(even, odd)] + [minus(e, o) for e, o in zip(even, odd)]


def matmul_pair(left, right, high, low):
    both = jnp.concatenate([left, right], axis=1)
    upper = both.astype(jnp.bfloat16)
    lower = (both - upper.astype(jnp.float32)).astype(jnp.bfloat16)
    product = functools.partial(jnp.dot, preferred_element_type=jnp.float32)
    result = product(upper, high) + (product(lower, high) + product(upper, low))
    return result[:, :LANES], result[:, LANES:]


def line_filter(field, filters, twist, high, low, sign):
    def stack(items, part):
        return jnp.concatenate([item[part] for item in items], axis=0)

    def pieces(real, imag):
        return [(real[k * CHUNK : (k + 1) * CHUNK], imag[k * CHUNK : (k + 1) * CHUNK]) for k in range(GROUPS)]

    multiply = times if sign > 0 else times_conj
    products = []
    for wave in field:
        for first in range(0, WIDE, CHUNK):
            parts = dft8([(real[first : first + CHUNK], imag[first : first + CHUNK]) for real, imag in wave], -1)
            parts = [parts[0]] + [times(parts[k], twist[k]) for k in range(1, GROUPS)]
            products.append(matmul_pair(stack(parts, 0), stack(parts, 1), high, low))
    returned = []
    for index, product in enumerate(products):
        picks = filters[index // (WIDE // CHUNK)]
        spectrum = [multiply(value, pick) for value, pick in zip(pieces(*product), picks)]
        imag, real = matmul_pair(stack(spectrum, 1), stack(spectrum, 0), high, low)
        returned.append((real, imag))
    chunks = []
    for product in returned:
        parts = pieces(*product)
        parts = [parts[0]] + [times_conj(parts[k], twist[k]) for k in range(1, GROUPS)]
        chunks.append(dft8(parts, 1))
    result = []
    for wave in range(len(field)):
        mine = chunks[wave * (WIDE // CHUNK) : (wave + 1) * (WIDE // CHUNK)]
        result.append(
            [
                tuple(jnp.concatenate([chunk[group][part] for chunk in mine], axis=0) for part in range(2))
                for group in range(GROUPS)
            ]
        )
    return result


def load_field(blocks_ref, start):
    turned = [
        jnp.concatenate([blocks_ref[GROUPS * i + j, start : start + WIDE] for i in range(FOLD)], axis=0).T
        for j in range(GROUPS)
    ]
    field = [[[None, None] for _ in range(GROUPS)] for _ in range(SHARE)]
    for part in range(2):
        for wave in range(SHARE):
            first = (part * SHARE + wave) * WIDE
            for half in range(GROUPS // FOLD):
                rows = [turned[half * FOLD + i][first : first + WIDE] for i in range(FOLD)]
                points = jnp.concatenate(rows, axis=0).T
                for i in range(FOLD):
                    group = i * (GROUPS // FOLD) + half
                    field[wave][group][part] = points[i * WIDE : (i + 1) * WIDE]
    return field


def store_field(blocks_ref, start, field):
    for group in range(GROUPS):
        rows = [field[w][group][part] for part in range(2) for w in range(SHARE)]
        turned = jnp.concatenate(rows, axis=0).T
        for i in range(FOLD):
            blocks_ref[FOLD * group + i, start : start + WIDE] = turned[i * WIDE : (i + 1) * WIDE]


def store_planes(blocks_ref, start, planes):
    lane = lax.broadcasted_iota(jnp.int32, (16, LANES), 1)
    for group in range(GROUPS):
        rows = [planes[0][group], planes[1][group]]
        turned = jnp.concatenate(rows + rows, axis=0).T
        for i in range(FOLD):
            upper, lower = turned[i * WIDE : i * WIDE + 16], turned[i * WIDE + 16 : (i + 1) * WIDE]
            blocks_ref[FOLD * group + i, start : start + 16] = jnp.where(lane < 64, upper, lower)


def load_planes(blocks_ref, start):
    turned = [
        jnp.concatenate([blocks_ref[FOLD * i + j, start : start + 16] for i in range(GROUPS)], axis=0).T
        for j in range(FOLD)
    ]
    planes = []
    for plane in range(2):
        halves = []
        for half in range(2):
            first = (half * 2 + plane) * WIDE
            halves.append(jnp.concatenate([t[first : first + WIDE] for t in turned], axis=0).T)
        planes.append(
            [
                jnp.concatenate([half[16 * group : 16 * (group + 1)] for half in halves], axis=0)
                for group in range(GROUPS)
            ]
        )
    return planes


def ratio_of(place_ref, wave):
    number = place_ref[2 + place_ref[0] * SHARE + wave]
    return ratio_base + ratio_step * number.astype(jnp.float32)


def write_constants(constants_ref, place_ref):
    row = lax.broadcasted_iota(jnp.int32, (GROUPS, LANES), 0)
    lane = lax.broadcasted_iota(jnp.int32, (GROUPS, LANES), 1)
    natural = row + GROUPS * lane
    signed = jnp.where(natural < GRID // 2, natural, natural - GRID)
    scaled = signed.astype(jnp.float32) * (2.0 / GRID)
    squares = scaled * scaled
    for wave in range(SHARE):
        ratio = ratio_of(place_ref, wave)
        real, imag = cos_sin((-prop_scale * ratio) * squares)
        constants_ref[2 * wave], constants_ref[2 * wave + 1] = real * (1.0 / GRID), imag * (1.0 / GRID)
        constants_ref[2 * SHARE + 2 + wave] = 1.0 / jnp.full((GROUPS, LANES), ratio, jnp.float32)
    constants_ref[3 * SHARE + 2] = jnp.full((GROUPS, LANES), place_ref[0].astype(jnp.float32), jnp.float32)
    real, imag = cos_sin((-2.0 * math.pi / GRID) * (row * lane).astype(jnp.float32))
    constants_ref[2 * SHARE], constants_ref[2 * SHARE + 1] = real, imag


class Constants:
    def __init__(self, constants_ref, high_ref, low_ref):
        def rows(real, imag):
            real, imag = constants_ref[real], constants_ref[imag]
            return [(real[k : k + 1], imag[k : k + 1]) for k in range(GROUPS)]

        self.filters = [rows(2 * wave, 2 * wave + 1) for wave in range(SHARE)]
        self.twist = rows(2 * SHARE, 2 * SHARE + 1)
        self.inverse = [constants_ref[2 * SHARE + 2 + wave][:1] for wave in range(SHARE)]
        self.high, self.low = high_ref[...], low_ref[...]

    def along(self, field, sign):
        return line_filter(field, self.filters, self.twist, self.high, self.low, sign)


def copies(pairs, sems):
    return [pltpu.make_async_copy(source, target, sems.at[i]) for i, (source, target) in enumerate(pairs)]


def start(moves):
    for move in moves:
        move.start()


def wait(moves):
    for move in moves:
        move.wait()


def launch_kernel(
    waves,
    place_ref,
    illum_hbm,
    high_hbm,
    low_hbm,
    measured_hbm,
    out_ref,
    target_ref,
    constants_ref,
    illum_ref,
    high_ref,
    low_ref,
    measured_ref,
    sems,
):
    own = measured_hbm.at[pl.ds(place_ref[0] * SHARE, SHARE)]
    moves = copies(
        [(illum_hbm, illum_ref), (high_hbm, high_ref), (low_hbm, low_ref), (own, measured_ref)], sems
    )
    start(moves)
    write_constants(constants_ref, place_ref)
    tilted = []
    for wave in range(SHARE):
        pick = place_ref[2 + waves + place_ref[0] * SHARE + wave]
        tilt_x = ((pick & (angle_side - 1)) - angle_side // 2) * tilt_step
        tilt_y = ((pick >> 3) - angle_side // 2) * tilt_step
        row = lax.broadcasted_iota(jnp.int32, (WIDE, LANES), 0) + place_ref[1] * WIDE

        def wheel(product):
            turned = ((product + GRID // 2) & (GRID - 1)) - GRID // 2
            return cos_sin((2.0 * math.pi / GRID) * turned.astype(jnp.float32))

        down = wheel(tilt_y * row)
        groups = []
        for group in range(GROUPS):
            column = lax.broadcasted_iota(jnp.int32, (8, LANES), 1) + group * LANES
            across = wheel(tilt_x * column)
            groups.append(times(down, (across[0][:1], across[1][:1])))
        tilted.append(groups)
    wait(moves[:3])
    field = []
    for wave in range(SHARE):
        groups = []
        for group in range(GROUPS):
            bright = illum_ref[:, group * LANES : (group + 1) * LANES]
            groups.append((bright * tilted[wave][group][0], bright * tilted[wave][group][1]))
        field.append(groups)
    store_field(out_ref, 0, Constants(constants_ref, high_ref, low_ref).along(field, 1))
    wait(moves[3:])
    for wave in range(SHARE):
        for part in range(2):
            target_ref[wave, part] = measured_ref[wave, :, part]


def save(kept_ref, field):
    for wave in range(SHARE):
        for group in range(GROUPS):
            for part in range(2):
                kept_ref[wave, group, part] = field[wave][group][part]


def kept(kept_ref):
    return [
        [(kept_ref[wave, group, 0], kept_ref[wave, group, 1]) for group in range(GROUPS)]
        for wave in range(SHARE)
    ]


def screens(base, constants):
    result = []
    for wave in range(SHARE):
        scale = constants.inverse[wave] * (2.0 / math.pi)
        result.append([cos_sin_quarters(plane * scale) for plane in base])
    return result


def gradient(target, field, constants):
    total = [None] * GROUPS
    for wave in range(SHARE):
        scale = constants.inverse[wave]
        for group in range(GROUPS):
            left, right = target[wave][group], field[wave][group]
            term = (left[0] * right[1] - left[1] * right[0]) * scale
            total[group] = term if wave == 0 else total[group] + term
    return total


def lanes_of(group):
    return slice(group * LANES, (group + 1) * LANES)


def planes_of(ref):
    return [ref[:, lanes_of(group)] for group in range(GROUPS)]


def target_of(target_ref):
    return [
        [(target_ref[wave, 0, :, lanes_of(group)], target_ref[wave, 1, :, lanes_of(group)]) for group in range(GROUPS)]
        for wave in range(SHARE)
    ]


def each(function, left, right):
    return [[function(a, b) for a, b in zip(p, q)] for p, q in zip(left, right)]


def begin_kernel(
    constants_ref,
    launched_ref,
    slice_0,
    slice_1,
    slice_2,
    slice_3,
    mask_ref,
    target_ref,
    high_ref,
    low_ref,
    out_ref,
    base_ref,
    screen_ref,
):
    constants = Constants(constants_ref, high_ref, low_ref)
    mask = [core_step * mask_ref[:, lanes_of(group)].astype(jnp.float32) for group in range(GROUPS)]

    def base_of(layer):
        back = constants_ref[3 * SHARE + 2][:1] - float(layer)
        back = jnp.where(back < 0.0, back + 4.0, back)
        result = []
        for group in range(GROUPS):
            value = slice_0[0, :, lanes_of(group)]
            for place, ref in enumerate((slice_1, slice_2, slice_3)):
                value = jnp.where(back == place + 1.0, ref[0, :, lanes_of(group)], value)
            result.append(mask[group] + value)
        return result

    for peer in range(PEERS):
        out_ref[peer, :WIDE] = launched_ref[peer]
    store_planes(out_ref, 2 * WIDE, (base_of(0), base_of(2)))
    for group, plane in enumerate(base_of(1)):
        base_ref[:, lanes_of(group)] = plane
    screen = screens(base_of(3), constants)
    save(screen_ref, screen)
    target = each(times_conj, target_of(target_ref), screen)
    store_field(out_ref, WIDE, constants.along(target, -1))


def first_kernel(constants_ref, in_ref, high_ref, low_ref, out_ref, field_ref, target_ref, screen_ref):
    constants = Constants(constants_ref, high_ref, low_ref)
    base_0, base_2 = load_planes(in_ref, 2 * WIDE)
    field = constants.along(load_field(in_ref, 0), 1)
    field = each(times, field, screens(base_0, constants))
    save(field_ref, field)
    store_field(out_ref, 0, constants.along(field, 1))
    target = constants.along(load_field(in_ref, WIDE), -1)
    save(target_ref, target)
    screen = screens(base_2, constants)
    save(screen_ref, screen)
    target = each(times_conj, target, screen)
    store_field(out_ref, WIDE, constants.along(target, -1))


def second_kernel(constants_ref, in_ref, high_ref, low_ref, base_ref, out_ref, grad_ref):
    constants = Constants(constants_ref, high_ref, low_ref)
    screen = screens(planes_of(base_ref), constants)
    field = constants.along(load_field(in_ref, 0), 1)
    field = each(times, field, screen)
    target = constants.along(load_field(in_ref, WIDE), -1)
    for group, plane in enumerate(gradient(target, field, constants)):
        grad_ref[:, lanes_of(group)] = plane
    store_field(out_ref, 0, constants.along(field, 1))
    target = each(times_conj, target, screen)
    store_field(out_ref, WIDE, constants.along(target, -1))


def third_kernel(constants_ref, in_ref, high_ref, low_ref, field_ref, target_ref, screen_ref, out_ref):
    constants = Constants(constants_ref, high_ref, low_ref)
    field = constants.along(load_field(in_ref, 0), 1)
    field = each(times, field, kept(screen_ref))
    grad_2 = gradient(kept(target_ref), field, constants)
    store_field(out_ref, 0, constants.along(field, 1))
    target = constants.along(load_field(in_ref, WIDE), -1)
    store_planes(out_ref, WIDE, (gradient(target, kept(field_ref), constants), grad_2))


def last_kernel(constants_ref, in_ref, high_ref, low_ref, screen_ref, target_ref, first_ref, *out_refs):
    constants = Constants(constants_ref, high_ref, low_ref)
    field = constants.along(load_field(in_ref, 0), 1)
    field = each(times, field, kept(screen_ref))
    grad_0, grad_2 = load_planes(in_ref, WIDE)
    planes = [grad_0, planes_of(first_ref), grad_2, gradient(target_of(target_ref), field, constants)]
    section = constants_ref[3 * SHARE + 2][:1]
    for place, out_ref in enumerate(out_refs):
        layer = section + float(place)
        layer = jnp.where(layer > 3.0, layer - 4.0, layer)
        for group in range(GROUPS):
            value = planes[0][group]
            for number in range(1, 4):
                value = jnp.where(layer == float(number), planes[number][group], value)
            out_ref[0, :, lanes_of(group)] = value


def sum_kernel(own_ref, one_ref, two_ref, three_ref, out_ref):
    out_ref[...] = (own_ref[...] + one_ref[...]) + (two_ref[...] + three_ref[...])


def call(kernel, scalars, near, far, outs, scratch=(), moves=1):
    specs = [pl.BlockSpec(memory_space=pltpu.SMEM)] * len(scalars)
    specs += [pl.BlockSpec(memory_space=pltpu.VMEM)] * len(near)
    specs += [pl.BlockSpec(memory_space=pltpu.HBM)] * len(far)
    scratch = [pltpu.VMEM(shape, dtype) for shape, dtype in scratch]
    if scratch:
        scratch.append(pltpu.SemaphoreType.DMA((moves,)))
    return pl.pallas_call(
        kernel,
        out_shape=[place(shape, jnp.float32) for shape, place in outs],
        in_specs=specs,
        out_specs=[pl.BlockSpec(memory_space=pltpu.VMEM)] * len(outs),
        scratch_shapes=scratch,
        compiler_params=pltpu.CompilerParams(vmem_limit_bytes=VMEM_LIMIT),
    )(*scalars, *near, *far)


def near(shape):
    return (shape, pltpu.VMEM)


def free(shape):
    return (shape, jax.ShapeDtypeStruct)


def in_hbm(*arrays):
    return tuple(pltpu.with_memory_space_constraint(array, pltpu.HBM) for array in arrays)


def body(index_slices, core_mask, illum_amp, measured, wave_ids, angle_ids):
    row_pos, sec_pos = lax.axis_index("row"), lax.axis_index("sec")
    sec_count, waves = lax.axis_size("sec"), wave_ids.shape[0]
    tables = tuple(jnp.asarray(table) for table in dft_tables())
    place = jnp.concatenate([sec_pos[None], row_pos[None], wave_ids, angle_ids]).astype(jnp.int32)
    swap = functools.partial(lax.all_to_all, split_axis=0, concat_axis=0, tiled=True)
    plane, saved = (WIDE, GRID), (SHARE, GROUPS, 2, WIDE, LANES)
    table = ((2 * LANES, 2 * LANES), jnp.bfloat16)

    def blocks(rows):
        return free((PEERS, rows, LANES))

    slices = [index_slices]
    for back in range(1, sec_count):
        pairs = [(i, (i + back) % sec_count) for i in range(sec_count)]
        slices.append(lax.ppermute(index_slices, "sec", pairs))
    launched, target, constants = call(
        functools.partial(launch_kernel, waves),
        (place,),
        (),
        in_hbm(illum_amp, *tables, measured),
        (near((PEERS, WIDE, LANES)), near((SHARE, 2, *plane)), near((3 * SHARE + 3, GROUPS, LANES))),
        scratch=((plane, jnp.float32), table, table, ((SHARE, *measured.shape[1:]), jnp.float32)),
        moves=4,
    )
    sent, base, screen_3 = call(
        begin_kernel,
        (),
        (constants, launched, *slices, core_mask, target, *tables),
        (),
        (blocks(2 * WIDE + 16), near(plane), near(saved)),
    )
    sent, field_0, target_2, screen_2 = call(
        first_kernel, (), (constants, swap(sent, "row"), *tables), (), (blocks(2 * WIDE),) + (near(saved),) * 3
    )
    sent, grad_1 = call(
        second_kernel, (), (constants, swap(sent, "row"), *tables, base), (), (blocks(2 * WIDE), near(plane))
    )
    (sent,) = call(
        third_kernel,
        (),
        (constants, swap(sent, "row"), *tables, field_0, target_2, screen_2),
        (),
        (blocks(WIDE + 16),),
    )
    grads = call(
        last_kernel,
        (),
        (constants, swap(sent, "row"), *tables, screen_3, target, grad_1),
        (),
        (free((1, *plane)),) * sec_count,
    )
    parts = [grads[0]]
    for on in range(1, sec_count):
        parts.append(lax.ppermute(grads[on], "sec", [(i, (i + on) % sec_count) for i in range(sec_count)]))
    (result,) = call(sum_kernel, (), parts, (), (free((1, *plane)),))
    return result


def solution(mesh):
    in_specs = (
        P("sec", "row", None),
        P("row", None),
        P("row", None),
        P(None, "row", None, None),
        P(),
        P(),
    )
    out_specs = P("sec", "row", None)
    return jax.shard_map(body, mesh=mesh, in_specs=in_specs, out_specs=out_specs, check_vma=False)
```

```python
import functools
import math

import jax
import jax.numpy as jnp
import numpy as np
from jax import lax
from jax.experimental import pallas as pl
from jax.experimental.pallas import tpu as pltpu
from jax.sharding import PartitionSpec as P

ratio_base = 0.75
ratio_step = 1.0 / 128.0
prop_scale = 150.0
core_step = 0.8
tilt_step = 8
angle_side = 8

LANES = 128
GROUPS = 8
GRID = GROUPS * LANES
WIDE = 32
PEERS = GRID // WIDE
SHARE = 2
FOLD = LANES // WIDE
CHUNK = 16
VMEM_LIMIT = 48 * 1024 * 1024


def dft_tables():
    counter = np.arange(LANES)
    angle = -2.0 * np.pi / LANES * (counter[:, None] * counter[None, :] % LANES)
    real, imag = np.cos(angle), np.sin(angle)
    full = np.block([[real, imag], [-imag, real]]).astype(np.float32)
    high = full.astype(jnp.bfloat16)
    low = (full - high.astype(np.float32)).astype(jnp.bfloat16)
    return high, low


def cos_sin(angle):
    turns = jnp.floor(angle * (2.0 / math.pi) + 0.5)
    rest = angle - turns * 1.5703125
    rest = rest - turns * 4.837512969970703e-4
    rest = rest - turns * 7.549789948768648e-8
    return in_quarter(turns, rest)


def cos_sin_quarters(quarters):
    turns = jnp.floor(quarters + 0.5)
    return in_quarter(turns, (quarters - turns) * (0.5 * math.pi))


def in_quarter(turns, rest):
    square = rest * rest
    sine = rest + rest * square * (
        -1.6666654611e-1 + square * (8.3321608736e-3 + square * -1.9515295891e-4)
    )
    cosine = (1.0 - 0.5 * square) + square * square * (
        4.166664568298827e-2 + square * (-1.388731625493765e-3 + square * 2.443315711809948e-5)
    )
    quarter = turns.astype(jnp.int32)
    swap = (quarter & 1) != 0
    cos_part = jnp.where(swap, sine, cosine)
    sin_part = jnp.where(swap, cosine, sine)
    cos_part = jnp.where(((quarter + 1) & 2) != 0, -cos_part, cos_part)
    sin_part = jnp.where((quarter & 2) != 0, -sin_part, sin_part)
    return cos_part, sin_part


def times(left, right):
    return (
        left[0] * right[0] - left[1] * right[1],
        left[0] * right[1] + left[1] * right[0],
    )


def times_conj(left, right):
    return (
        left[0] * right[0] + left[1] * right[1],
        left[1] * right[0] - left[0] * right[1],
    )


def plus(left, right):
    return (left[0] + right[0], left[1] + right[1])


def minus(left, right):
    return (left[0] - right[0], left[1] - right[1])


def quarter_turn(value, sign):
    if sign > 0:
        return (-value[1], value[0])
    return (value[1], -value[0])


def dft4(items, sign):
    even, odd = plus(items[0], items[2]), minus(items[0], items[2])
    other, rest = plus(items[1], items[3]), minus(items[1], items[3])
    rest = quarter_turn(rest, sign)
    return [plus(even, other), plus(odd, rest), minus(even, other), minus(odd, rest)]


def dft8(items, sign):
    even, odd = dft4(items[0::2], sign), dft4(items[1::2], sign)
    half = math.sqrt(0.5)
    first, third = odd[1], odd[3]
    if sign > 0:
        first = ((first[0] - first[1]) * half, (first[0] + first[1]) * half)
        third = ((-third[0] - third[1]) * half, (third[0] - third[1]) * half)
    else:
        first = ((first[0] + first[1]) * half, (first[1] - first[0]) * half)
        third = ((third[1] - third[0]) * half, (-third[0] - third[1]) * half)
    odd = [odd[0], first, quarter_turn(odd[2], sign), third]
    return [plus(e, o) for e, o in zip(even, odd)] + [minus(e, o) for e, o in zip(even, odd)]


def matmul_pair(left, right, high, low):
    both = jnp.concatenate([left, right], axis=1)
    upper = both.astype(jnp.bfloat16)
    lower = (both - upper.astype(jnp.float32)).astype(jnp.bfloat16)
    product = functools.partial(jnp.dot, preferred_element_type=jnp.float32)
    result = product(upper, high) + (product(lower, high) + product(upper, low))
    return result[:, :LANES], result[:, LANES:]


def line_filter(field, filters, twist, high, low, sign):
    def stack(items, part):
        return jnp.concatenate([item[part] for item in items], axis=0)

    def pieces(real, imag):
        return [(real[k * CHUNK : (k + 1) * CHUNK], imag[k * CHUNK : (k + 1) * CHUNK]) for k in range(GROUPS)]

    multiply = times if sign > 0 else times_conj
    products = []
    for wave in field:
        for first in range(0, WIDE, CHUNK):
            parts = dft8([(real[first : first + CHUNK], imag[first : first + CHUNK]) for real, imag in wave], -1)
            parts = [parts[0]] + [times(parts[k], twist[k]) for k in range(1, GROUPS)]
            products.append(matmul_pair(stack(parts, 0), stack(parts, 1), high, low))
    returned = []
    for index, product in enumerate(products):
        picks = filters[index // (WIDE // CHUNK)]
        spectrum = [multiply(value, pick) for value, pick in zip(pieces(*product), picks)]
        imag, real = matmul_pair(stack(spectrum, 1), stack(spectrum, 0), high, low)
        returned.append((real, imag))
    chunks = []
    for product in returned:
        parts = pieces(*product)
        parts = [parts[0]] + [times_conj(parts[k], twist[k]) for k in range(1, GROUPS)]
        chunks.append(dft8(parts, 1))
    result = []
    for wave in range(len(field)):
        mine = chunks[wave * (WIDE // CHUNK) : (wave + 1) * (WIDE // CHUNK)]
        result.append(
            [
                tuple(jnp.concatenate([chunk[group][part] for chunk in mine], axis=0) for part in range(2))
                for group in range(GROUPS)
            ]
        )
    return result


def load_field(blocks_ref, start):
    turned = [
        jnp.concatenate([blocks_ref[GROUPS * i + j, start : start + WIDE] for i in range(FOLD)], axis=0).T
        for j in range(GROUPS)
    ]
    field = [[[None, None] for _ in range(GROUPS)] for _ in range(SHARE)]
    for part in range(2):
        for wave in range(SHARE):
            first = (part * SHARE + wave) * WIDE
            for half in range(GROUPS // FOLD):
                rows = [turned[half * FOLD + i][first : first + WIDE] for i in range(FOLD)]
                points = jnp.concatenate(rows, axis=0).T
                for i in range(FOLD):
                    group = i * (GROUPS // FOLD) + half
                    field[wave][group][part] = points[i * WIDE : (i + 1) * WIDE]
    return field


def store_field(blocks_ref, start, field):
    for group in range(GROUPS):
        rows = [field[w][group][part] for part in range(2) for w in range(SHARE)]
        turned = jnp.concatenate(rows, axis=0).T
        for i in range(FOLD):
            blocks_ref[FOLD * group + i, start : start + WIDE] = turned[i * WIDE : (i + 1) * WIDE]


def store_planes(blocks_ref, start, planes):
    lane = lax.broadcasted_iota(jnp.int32, (16, LANES), 1)
    for group in range(GROUPS):
        rows = [planes[0][group], planes[1][group]]
        turned = jnp.concatenate(rows + rows, axis=0).T
        for i in range(FOLD):
            upper, lower = turned[i * WIDE : i * WIDE + 16], turned[i * WIDE + 16 : (i + 1) * WIDE]
            blocks_ref[FOLD * group + i, start : start + 16] = jnp.where(lane < 64, upper, lower)


def load_planes(blocks_ref, start):
    turned = [
        jnp.concatenate([blocks_ref[FOLD * i + j, start : start + 16] for i in range(GROUPS)], axis=0).T
        for j in range(FOLD)
    ]
    planes = []
    for plane in range(2):
        halves = []
        for half in range(2):
            first = (half * 2 + plane) * WIDE
            halves.append(jnp.concatenate([t[first : first + WIDE] for t in turned], axis=0).T)
        planes.append(
            [
                jnp.concatenate([half[16 * group : 16 * (group + 1)] for half in halves], axis=0)
                for group in range(GROUPS)
            ]
        )
    return planes


def ratio_of(place_ref, wave):
    number = place_ref[2 + place_ref[0] * SHARE + wave]
    return ratio_base + ratio_step * number.astype(jnp.float32)


def write_constants(constants_ref, place_ref):
    row = lax.broadcasted_iota(jnp.int32, (GROUPS, LANES), 0)
    lane = lax.broadcasted_iota(jnp.int32, (GROUPS, LANES), 1)
    natural = row + GROUPS * lane
    signed = jnp.where(natural < GRID // 2, natural, natural - GRID)
    scaled = signed.astype(jnp.float32) * (2.0 / GRID)
    squares = scaled * scaled
    for wave in range(SHARE):
        ratio = ratio_of(place_ref, wave)
        real, imag = cos_sin((-prop_scale * ratio) * squares)
        constants_ref[2 * wave], constants_ref[2 * wave + 1] = real * (1.0 / GRID), imag * (1.0 / GRID)
        constants_ref[2 * SHARE + 2 + wave] = 1.0 / jnp.full((GROUPS, LANES), ratio, jnp.float32)
    constants_ref[3 * SHARE + 2] = jnp.full((GROUPS, LANES), place_ref[0].astype(jnp.float32), jnp.float32)
    real, imag = cos_sin((-2.0 * math.pi / GRID) * (row * lane).astype(jnp.float32))
    constants_ref[2 * SHARE], constants_ref[2 * SHARE + 1] = real, imag


class Constants:
    def __init__(self, constants_ref, high_ref, low_ref):
        def rows(real, imag):
            real, imag = constants_ref[real], constants_ref[imag]
            return [(real[k : k + 1], imag[k : k + 1]) for k in range(GROUPS)]

        self.filters = [rows(2 * wave, 2 * wave + 1) for wave in range(SHARE)]
        self.twist = rows(2 * SHARE, 2 * SHARE + 1)
        self.inverse = [constants_ref[2 * SHARE + 2 + wave][:1] for wave in range(SHARE)]
        self.high, self.low = high_ref[...], low_ref[...]

    def along(self, field, sign):
        return line_filter(field, self.filters, self.twist, self.high, self.low, sign)


def copies(pairs, sems):
    return [pltpu.make_async_copy(source, target, sems.at[i]) for i, (source, target) in enumerate(pairs)]


def start(moves):
    for move in moves:
        move.start()


def wait(moves):
    for move in moves:
        move.wait()


def launch_kernel(
    waves,
    place_ref,
    illum_hbm,
    high_hbm,
    low_hbm,
    measured_hbm,
    out_ref,
    target_ref,
    constants_ref,
    illum_ref,
    high_ref,
    low_ref,
    measured_ref,
    sems,
):
    own = measured_hbm.at[pl.ds(place_ref[0] * SHARE, SHARE)]
    moves = copies(
        [(illum_hbm, illum_ref), (high_hbm, high_ref), (low_hbm, low_ref), (own, measured_ref)], sems
    )
    start(moves)
    write_constants(constants_ref, place_ref)
    tilted = []
    for wave in range(SHARE):
        pick = place_ref[2 + waves + place_ref[0] * SHARE + wave]
        tilt_x = ((pick & (angle_side - 1)) - angle_side // 2) * tilt_step
        tilt_y = ((pick >> 3) - angle_side // 2) * tilt_step
        row = lax.broadcasted_iota(jnp.int32, (WIDE, LANES), 0) + place_ref[1] * WIDE

        def wheel(product):
            turned = ((product + GRID // 2) & (GRID - 1)) - GRID // 2
            return cos_sin((2.0 * math.pi / GRID) * turned.astype(jnp.float32))

        down = wheel(tilt_y * row)
        groups = []
        for group in range(GROUPS):
            column = lax.broadcasted_iota(jnp.int32, (8, LANES), 1) + group * LANES
            across = wheel(tilt_x * column)
            groups.append(times(down, (across[0][:1], across[1][:1])))
        tilted.append(groups)
    wait(moves[:3])
    field = []
    for wave in range(SHARE):
        groups = []
        for group in range(GROUPS):
            bright = illum_ref[:, group * LANES : (group + 1) * LANES]
            groups.append((bright * tilted[wave][group][0], bright * tilted[wave][group][1]))
        field.append(groups)
    store_field(out_ref, 0, Constants(constants_ref, high_ref, low_ref).along(field, 1))
    wait(moves[3:])
    for wave in range(SHARE):
        for part in range(2):
            target_ref[wave, part] = measured_ref[wave, :, part]


def save(kept_ref, field):
    for wave in range(SHARE):
        for group in range(GROUPS):
            for part in range(2):
                kept_ref[wave, group, part] = field[wave][group][part]


def kept(kept_ref):
    return [
        [(kept_ref[wave, group, 0], kept_ref[wave, group, 1]) for group in range(GROUPS)]
        for wave in range(SHARE)
    ]


def screens(base, constants):
    result = []
    for wave in range(SHARE):
        scale = constants.inverse[wave] * (2.0 / math.pi)
        result.append([cos_sin_quarters(plane * scale) for plane in base])
    return result


def gradient(target, field, constants):
    total = [None] * GROUPS
    for wave in range(SHARE):
        scale = constants.inverse[wave]
        for group in range(GROUPS):
            left, right = target[wave][group], field[wave][group]
            term = (left[0] * right[1] - left[1] * right[0]) * scale
            total[group] = term if wave == 0 else total[group] + term
    return total


def lanes_of(group):
    return slice(group * LANES, (group + 1) * LANES)


def planes_of(ref):
    return [ref[:, lanes_of(group)] for group in range(GROUPS)]


def target_of(target_ref):
    return [
        [(target_ref[wave, 0, :, lanes_of(group)], target_ref[wave, 1, :, lanes_of(group)]) for group in range(GROUPS)]
        for wave in range(SHARE)
    ]


def each(function, left, right):
    return [[function(a, b) for a, b in zip(p, q)] for p, q in zip(left, right)]


def begin_kernel(
    constants_ref,
    launched_ref,
    slice_0,
    slice_1,
    slice_2,
    slice_3,
    mask_ref,
    target_ref,
    high_ref,
    low_ref,
    out_ref,
    base_ref,
    screen_ref,
):
    constants = Constants(constants_ref, high_ref, low_ref)
    mask = [core_step * mask_ref[:, lanes_of(group)].astype(jnp.float32) for group in range(GROUPS)]

    def base_of(layer):
        back = constants_ref[3 * SHARE + 2][:1] - float(layer)
        back = jnp.where(back < 0.0, back + 4.0, back)
        result = []
        for group in range(GROUPS):
            value = slice_0[0, :, lanes_of(group)]
            for place, ref in enumerate((slice_1, slice_2, slice_3)):
                value = jnp.where(back == place + 1.0, ref[0, :, lanes_of(group)], value)
            result.append(mask[group] + value)
        return result

    for peer in range(PEERS):
        out_ref[peer, :WIDE] = launched_ref[peer]
    store_planes(out_ref, 2 * WIDE, (base_of(0), base_of(2)))
    for group, plane in enumerate(base_of(1)):
        base_ref[:, lanes_of(group)] = plane
    screen = screens(base_of(3), constants)
    save(screen_ref, screen)
    target = each(times_conj, target_of(target_ref), screen)
    store_field(out_ref, WIDE, constants.along(target, -1))


def first_kernel(constants_ref, in_ref, high_ref, low_ref, out_ref, field_ref, target_ref, screen_ref):
    constants = Constants(constants_ref, high_ref, low_ref)
    base_0, base_2 = load_planes(in_ref, 2 * WIDE)
    field = constants.along(load_field(in_ref, 0), 1)
    field = each(times, field, screens(base_0, constants))
    save(field_ref, field)
    store_field(out_ref, 0, constants.along(field, 1))
    target = constants.along(load_field(in_ref, WIDE), -1)
    save(target_ref, target)
    screen = screens(base_2, constants)
    save(screen_ref, screen)
    target = each(times_conj, target, screen)
    store_field(out_ref, WIDE, constants.along(target, -1))


def second_kernel(constants_ref, in_ref, high_ref, low_ref, base_ref, out_ref, grad_ref):
    constants = Constants(constants_ref, high_ref, low_ref)
    screen = screens(planes_of(base_ref), constants)
    field = constants.along(load_field(in_ref, 0), 1)
    field = each(times, field, screen)
    target = constants.along(load_field(in_ref, WIDE), -1)
    for group, plane in enumerate(gradient(target, field, constants)):
        grad_ref[:, lanes_of(group)] = plane
    store_field(out_ref, 0, constants.along(field, 1))
    target = each(times_conj, target, screen)
    store_field(out_ref, WIDE, constants.along(target, -1))


def third_kernel(constants_ref, in_ref, high_ref, low_ref, field_ref, target_ref, screen_ref, out_ref):
    constants = Constants(constants_ref, high_ref, low_ref)
    field = constants.along(load_field(in_ref, 0), 1)
    field = each(times, field, kept(screen_ref))
    grad_2 = gradient(kept(target_ref), field, constants)
    store_field(out_ref, 0, constants.along(field, 1))
    target = constants.along(load_field(in_ref, WIDE), -1)
    store_planes(out_ref, WIDE, (gradient(target, kept(field_ref), constants), grad_2))


def last_kernel(constants_ref, in_ref, high_ref, low_ref, screen_ref, target_ref, first_ref, *out_refs):
    constants = Constants(constants_ref, high_ref, low_ref)
    field = constants.along(load_field(in_ref, 0), 1)
    field = each(times, field, kept(screen_ref))
    grad_0, grad_2 = load_planes(in_ref, WIDE)
    planes = [grad_0, planes_of(first_ref), grad_2, gradient(target_of(target_ref), field, constants)]
    section = constants_ref[3 * SHARE + 2][:1]
    for place, out_ref in enumerate(out_refs):
        layer = section + float(place)
        layer = jnp.where(layer > 3.0, layer - 4.0, layer)
        for group in range(GROUPS):
            value = planes[0][group]
            for number in range(1, 4):
                value = jnp.where(layer == float(number), planes[number][group], value)
            out_ref[0, :, lanes_of(group)] = value


def sum_kernel(own_ref, one_ref, two_ref, three_ref, out_ref):
    out_ref[...] = (own_ref[...] + one_ref[...]) + (two_ref[...] + three_ref[...])


def call(kernel, scalars, near, far, outs, scratch=(), moves=1):
    specs = [pl.BlockSpec(memory_space=pltpu.SMEM)] * len(scalars)
    specs += [pl.BlockSpec(memory_space=pltpu.VMEM)] * len(near)
    specs += [pl.BlockSpec(memory_space=pltpu.HBM)] * len(far)
    scratch = [pltpu.VMEM(shape, dtype) for shape, dtype in scratch]
    if scratch:
        scratch.append(pltpu.SemaphoreType.DMA((moves,)))
    return pl.pallas_call(
        kernel,
        out_shape=[place(shape, jnp.float32) for shape, place in outs],
        in_specs=specs,
        out_specs=[pl.BlockSpec(memory_space=pltpu.VMEM)] * len(outs),
        scratch_shapes=scratch,
        compiler_params=pltpu.CompilerParams(vmem_limit_bytes=VMEM_LIMIT),
    )(*scalars, *near, *far)


def near(shape):
    return (shape, pltpu.VMEM)


def free(shape):
    return (shape, jax.ShapeDtypeStruct)


def in_hbm(*arrays):
    return tuple(pltpu.with_memory_space_constraint(array, pltpu.HBM) for array in arrays)


def body(index_slices, core_mask, illum_amp, measured, wave_ids, angle_ids):
    row_pos, sec_pos = lax.axis_index("row"), lax.axis_index("sec")
    sec_count, waves = lax.axis_size("sec"), wave_ids.shape[0]
    tables = tuple(jnp.asarray(table) for table in dft_tables())
    place = jnp.concatenate([sec_pos[None], row_pos[None], wave_ids, angle_ids]).astype(jnp.int32)
    swap = functools.partial(lax.all_to_all, split_axis=0, concat_axis=0, tiled=True)
    plane, saved = (WIDE, GRID), (SHARE, GROUPS, 2, WIDE, LANES)
    table = ((2 * LANES, 2 * LANES), jnp.bfloat16)

    def blocks(rows):
        return free((PEERS, rows, LANES))

    slices = [index_slices]
    for back in range(1, sec_count):
        pairs = [(i, (i + back) % sec_count) for i in range(sec_count)]
        slices.append(lax.ppermute(index_slices, "sec", pairs))
    launched, target, constants = call(
        functools.partial(launch_kernel, waves),
        (place,),
        (),
        in_hbm(illum_amp, *tables, measured),
        (near((PEERS, WIDE, LANES)), near((SHARE, 2, *plane)), near((3 * SHARE + 3, GROUPS, LANES))),
        scratch=((plane, jnp.float32), table, table, ((SHARE, *measured.shape[1:]), jnp.float32)),
        moves=4,
    )
    sent, base, screen_3 = call(
        begin_kernel,
        (),
        (constants, launched, *slices, core_mask, target, *tables),
        (),
        (blocks(2 * WIDE + 16), near(plane), near(saved)),
    )
    sent, field_0, target_2, screen_2 = call(
        first_kernel, (), (constants, swap(sent, "row"), *tables), (), (blocks(2 * WIDE),) + (near(saved),) * 3
    )
    sent, grad_1 = call(
        second_kernel, (), (constants, swap(sent, "row"), *tables, base), (), (blocks(2 * WIDE), near(plane))
    )
    (sent,) = call(
        third_kernel,
        (),
        (constants, swap(sent, "row"), *tables, field_0, target_2, screen_2),
        (),
        (blocks(WIDE + 16),),
    )
    grads = call(
        last_kernel,
        (),
        (constants, swap(sent, "row"), *tables, screen_3, target, grad_1),
        (),
        (free((1, *plane)),) * sec_count,
    )
    parts = [grads[0]]
    for on in (2, 1, 3):
        parts.append(lax.ppermute(grads[on], "sec", [(i, (i + on) % sec_count) for i in range(sec_count)]))
    (result,) = call(sum_kernel, (), parts, (), (free((1, *plane)),))
    return result


def solution(mesh):
    in_specs = (
        P("sec", "row", None),
        P("row", None),
        P("row", None),
        P(None, "row", None, None),
        P(),
        P(),
    )
    out_specs = P("sec", "row", None)
    return jax.shard_map(body, mesh=mesh, in_specs=in_specs, out_specs=out_specs, check_vma=False)
```
